256 devices in a mesh: pipe: 8 (over y, core), space: 32 (over x, z).
Axes of the slice: x: 4, y: 4, z: 8, core: 2. Of those that a mesh axis runs over, the one named last changes fastest.
Arguments:
- activations: bfloat16 [8, 64, 128, 2048], P('pipe', 'space'), may hold values from -6 to 6
- cotangent: bfloat16 [64, 128, 2048], P('space'), may hold values from -6 to 6
- w_first: bfloat16 [8, 2, 8, 256, 256], P('pipe'), may hold values from -0.25 to 0.25
- w_second: bfloat16 [8, 2, 8, 256, 256], P('pipe'), may hold values from -0.25 to 0.25
- b_first: float32 [8, 2, 2048], P('pipe'), may hold values from -1 to 1
Outputs:
- grads: bfloat16 [8, 64, 128, 2048], P('pipe', 'space')
The draws below stay inside these ranges and needn't reach their ends.
All inputs are finite; a program needn't handle non-finite values.
Results may differ from the reference program's by a relative error of at most 0.028.
Values may be sent and summed in bfloat16 or wider, within the bound.
No kernel may reach another device: no remote copies, remote signals or barrier semaphores. Data moves between devices by JAX's collectives and lax.ppermute only.
A program may use at most 64 MiB of HBM per device.

```python
import jax
import jax.numpy as jnp
from jax import lax

H = 64
W = 128
NB = 8
BS = 256
C = 2048
SEGMENTS = 8


def shard_levels(stream_key, shape, cuts, smallest, high):
    def one(dim, blocks):
        steps = jax.random.uniform(jax.random.fold_in(jax.random.fold_in(stream_key, 6), dim), (blocks,), jnp.float32, smallest / len(cuts), high / len(cuts))
        return jnp.repeat(jnp.exp(steps), shape[dim] // blocks).reshape((-1,) + (1,) * (len(shape) - dim - 1))

    loudness = one(*cuts[0])
    for cut in cuts[1:]:
        loudness = loudness * one(*cut)
    return loudness


def bell_draw(own_key, dims, scale, most, shards=(), held_as=jnp.bfloat16):
    loudness = shard_levels(own_key, dims, shards, -0.22, 0.18) if shards else 1.0
    drawn = jax.random.normal(own_key, dims, jnp.float32) * scale * loudness
    return jnp.minimum(jnp.maximum(drawn, -most), most).astype(held_as)


def setup_inputs(seed: int = 0) -> dict:
    keys = jax.random.split(jax.random.key(seed), 6)
    return {
        "activations": bell_draw(keys[0], (SEGMENTS, H, W, C), 1.0, 6.0, ((0, 8), (1, 32))),
        "cotangent": bell_draw(keys[1], (H, W, C), 1.0, 6.0, ((0, 32),)),
        "w_first": bell_draw(keys[2], (SEGMENTS, 2, NB, BS, BS), (2 * BS) ** -0.5, 0.25, ((0, 8),)),
        "w_second": bell_draw(keys[3], (SEGMENTS, 2, NB, BS, BS), (2 * BS) ** -0.5, 0.25, ((0, 8),)),
        "b_first": jnp.clip(jax.random.uniform(keys[4], (SEGMENTS, 2, C), jnp.float32, -1.0, 1.0) * shard_levels(keys[4], (SEGMENTS, 2, C), ((0, 8),), -0.4, 0.0), -1.0, 1.0),
    }


def gelu_slope(values):
    return 0.5 * (1.0 + lax.erf(values * 0.7071067811865476)) + values * jnp.exp(-0.5 * values * values) * 0.3989422804014327


def spectrum(field_values, doubled):
    mode_count = W // 2
    along_rows = jnp.fft.rfft(field_values, axis=1, norm="ortho")[:, :mode_count]
    if doubled:
        factor = jnp.where(jnp.arange(mode_count) == 0, 1.0, 2.0).astype(jnp.float32)
        joined = along_rows * factor[None, :, None]
    else:
        part_real, part_imag = lax.optimization_barrier((jnp.real(along_rows).astype(jnp.bfloat16), jnp.imag(along_rows).astype(jnp.bfloat16)))
        joined = lax.complex(part_real.astype(jnp.float32), part_imag.astype(jnp.float32))
    full_modes = jnp.fft.fft(joined, axis=0, norm="ortho")
    return jnp.real(full_modes).astype(jnp.bfloat16), jnp.imag(full_modes).astype(jnp.bfloat16)


def inverse(grad_real, grad_imag):
    joined = lax.complex(grad_real.astype(jnp.float32), grad_imag.astype(jnp.float32))
    along_height = jnp.fft.ifft(joined, axis=0, norm="ortho")
    part_real, part_imag = lax.optimization_barrier((jnp.real(along_height).astype(jnp.bfloat16), jnp.imag(along_height).astype(jnp.bfloat16)))
    rejoined = lax.complex(part_real.astype(jnp.float32), part_imag.astype(jnp.float32))
    padded = jnp.pad(rejoined, ((0, 0), (0, W - W // 2), (0, 0)))
    return jnp.real(jnp.fft.ifft(padded, axis=1, norm="ortho"))


def blocked(operand, weights, transposed):
    pattern = "tnk,njk->tnj" if transposed else "tnj,njk->tnk"
    return jnp.einsum(pattern, operand.astype(jnp.float32), weights.astype(jnp.float32), precision=lax.Precision.HIGHEST)


def segment_back(activation, gradient, layer_one, layer_two, bias_one):
    token_count = H * (W // 2)
    spec_real, spec_imag = spectrum(activation.astype(jnp.float32), False)
    grad_real, grad_imag = spectrum(gradient, True)

    def to_tokens(values):
        return values.reshape(token_count, NB, BS)

    spec_real, spec_imag = to_tokens(spec_real), to_tokens(spec_imag)
    grad_real, grad_imag = to_tokens(grad_real), to_tokens(grad_imag)
    z_real = blocked(spec_real, layer_one[0], False) - blocked(spec_imag, layer_one[1], False) + bias_one[0].reshape(NB, BS)
    z_imag = blocked(spec_real, layer_one[1], False) + blocked(spec_imag, layer_one[0], False) + bias_one[1].reshape(NB, BS)
    adj_real = blocked(grad_real, layer_two[0], True) + blocked(grad_imag, layer_two[1], True)
    adj_imag = blocked(grad_imag, layer_two[0], True) - blocked(grad_real, layer_two[1], True)
    pre_real = (adj_real * gelu_slope(z_real)).astype(jnp.bfloat16)
    pre_imag = (adj_imag * gelu_slope(z_imag)).astype(jnp.bfloat16)
    src_real = (blocked(pre_real, layer_one[0], True) + blocked(pre_imag, layer_one[1], True)).astype(jnp.bfloat16)
    src_imag = (blocked(pre_imag, layer_one[0], True) - blocked(pre_real, layer_one[1], True)).astype(jnp.bfloat16)
    spatial = inverse(src_real.reshape(H, W // 2, NB * BS), src_imag.reshape(H, W // 2, NB * BS))
    return spatial + gradient


def reference(activations, cotangent, w_first, w_second, b_first):
    gradient = cotangent.astype(jnp.float32)
    collected = []
    for segment_index in range(SEGMENTS - 1, -1, -1):
        gradient = segment_back(activations[segment_index], gradient, w_first[segment_index], w_second[segment_index], b_first[segment_index])
        collected.append(gradient.astype(jnp.bfloat16))
    return jnp.stack(collected[::-1])
```

```python
import math

import jax
import jax.numpy as jnp
import numpy as np
from jax import lax
from jax.experimental import pallas as pl
from jax.experimental.pallas import tpu as pltpu
from jax.sharding import PartitionSpec as P


BF16 = jnp.bfloat16
F32 = jnp.float32


def two_parts(table):
    high = table.astype(np.float32).astype(BF16)
    low = (table - high.astype(np.float64)).astype(np.float32).astype(BF16)
    return np.concatenate([high, low], axis=1)


def row_matrix(rows, width, columns, doubled):
    modes = width // 2
    pair = modes // columns
    angles = 2.0 * math.pi * (np.outer(np.arange(modes), np.arange(width)) % width) / width
    scale = 1.0 / math.sqrt(width)
    factor = np.where(np.arange(modes) == 0, 1.0, 2.0)[:, None] if doubled else 1.0
    parts = np.stack([np.cos(angles), -np.sin(angles)]) * scale * factor
    table = np.zeros((columns, rows, 2, pair, rows, width))
    by_column = parts.reshape(2, columns, pair, width).transpose(1, 0, 2, 3)
    for h in range(rows):
        table[:, h, :, :, h, :] = by_column
    return table.reshape(columns * rows * 2 * pair, rows * width)


def column_matrix(height, pair):
    angles = 2.0 * math.pi * (np.outer(np.arange(height), np.arange(height)) % height) / height
    scale = 1.0 / math.sqrt(height)
    cosines, sines = np.cos(angles) * scale, np.sin(angles) * scale
    table = np.zeros((2, pair, height, height, 2, pair))
    for k in range(pair):
        table[0, k, :, :, 0, k] = cosines
        table[0, k, :, :, 1, k] = sines
        table[1, k, :, :, 1, k] = cosines
        table[1, k, :, :, 0, k] = -sines
    return table.reshape(2 * pair * height, 2 * pair * height)


def fold_matrices(height, pair):
    size = 2 * pair * height
    plain = np.eye(size)
    folded = np.eye(size).reshape(2, pair, height, 2, pair, height)
    eye = np.eye(height)
    flip = eye[(-np.arange(height)) % height]
    folded[0, 0, :, 0, 0, :] = 0.5 * (eye + flip)
    folded[1, 0, :, 1, 0, :] = 0.5 * (eye - flip)
    return np.stack([plain, folded.reshape(size, size)]).astype(np.float32).astype(BF16)


def dot(left, right):
    return jnp.dot(left, right, preferred_element_type=F32)


def dot_t(left, right):
    return lax.dot_general(left, right, (((1,), (1,)), ((), ())), preferred_element_type=F32)


def gelu_slope(values):
    return (
        0.5 * (1.0 + lax.erf(values * 0.7071067811865476))
        + values * jnp.exp(-0.5 * values * values) * 0.3989422804014327
    )


def twice(table_ref, operand):
    depth = operand.shape[0]
    return dot(table_ref[:, :depth], operand) + dot(table_ref[:, depth:], operand)


def row_kernel(table_ref, act_ref, out_ref):
    out_ref[0] = twice(table_ref, act_ref[...]).astype(BF16)


def inverse_kernel(table_ref, spec_ref, cot_ref, out_ref):
    out_ref[...] = (twice(table_ref, spec_ref[0]) + cot_ref[...].astype(F32)).astype(BF16)


def chain_kernel(me_ref, act_ref, grad_ref, col_ref, inv_ref, fold_ref, *rest):
    sections = act_ref.shape[0]
    weights = rest[:sections]
    out_ref, held, sems = rest[sections:]
    size = act_ref.shape[2]
    half = act_ref.shape[1] // 2
    me = me_ref[0]
    copies = []
    for d in range(sections):
        slot = lax.rem(me - d + sections, sections)
        copy = pltpu.make_async_copy(weights[d], held.at[slot], sems.at[d])
        copy.start()
        copies.append(copy)

    base = twice(col_ref, grad_ref[...])
    total = jnp.zeros_like(base)
    height_total = jnp.zeros_like(base)
    grad = base.astype(BF16)
    spectra = [twice(col_ref, act_ref[p]).astype(BF16) for p in range(sections)]
    for copy in copies:
        copy.wait()

    for p in range(sections - 1, -1, -1):
        a_re, a_im = held[p, 0:size], held[p, size : 2 * size]
        b_re, b_im = held[p, 2 * size : 3 * size], held[p, 3 * size : 4 * size]
        bias = held[p, 4 * size : 4 * size + 16].astype(F32)
        bias_re = bias[0:1] + bias[1:2] + bias[2:3]
        bias_im = bias[8:9] + bias[9:10] + bias[10:11]
        s = spectra[p]
        s_turned = jnp.concatenate([-s[half:], s[:half]], axis=0)
        z = dot(s, a_re) + dot(s_turned, a_im)
        z = jnp.concatenate([z[:half] + bias_re, z[half:] + bias_im], axis=0)
        slope = gelu_slope(z)
        g_turned = jnp.concatenate([grad[half:], -grad[:half]], axis=0)
        u = dot_t(grad, b_re) + dot_t(g_turned, b_im)
        q = (u * slope).astype(BF16)
        q_turned = jnp.concatenate([q[half:], -q[:half]], axis=0)
        e = (dot_t(q, a_re) + dot_t(q_turned, a_im)).astype(BF16)
        height_total = height_total + twice(inv_ref, e)
        out_ref[p] = height_total.astype(BF16)
        if p > 0:
            total = total + dot(fold_ref[0], e)
            grad = (base + total).astype(BF16)


def body(activations, cotangent, w_first, w_second, b_first):
    sections = lax.axis_size("pipe")
    columns = lax.axis_size("space")
    me = lax.axis_index("pipe")
    here = lax.axis_index("space")
    _, rows, width, channels = activations.shape
    blocks, size = w_first.shape[2], w_first.shape[3]
    height = rows * columns
    pair = width // 2 // columns
    count = 2 * rows * width // 2
    tile = 2 * rows * pair
    forward_rows = two_parts(row_matrix(rows, width, columns, False))
    forward_rows_doubled = two_parts(row_matrix(rows, width, columns, True))
    inverse_rows = two_parts(row_matrix(rows, width, columns, False).T)
    forward_columns = two_parts(column_matrix(height, pair))
    inverse_columns = two_parts(column_matrix(height, pair).T)
    folds = fold_matrices(height, pair)

    first, second, bias = w_first[0], w_second[0], b_first[0]
    bias_high = lax.reduce_precision(bias, 8, 7)
    bias_mid = lax.reduce_precision(bias - bias_high, 8, 7)
    bias_low = bias - bias_high - bias_mid
    bias_parts = jnp.stack([bias_high, bias_mid, bias_low], axis=1)
    bias_parts = jnp.pad(bias_parts, ((0, 0), (0, 5), (0, 0))).astype(BF16).reshape(16, channels)
    pieces = []
    for d in range(sections):
        block = lax.rem(me + d, sections)
        piece = jnp.concatenate(
            [
                lax.dynamic_index_in_dim(first, block, 1, keepdims=False).reshape(2 * size, size),
                lax.dynamic_index_in_dim(second, block, 1, keepdims=False).reshape(2 * size, size),
                lax.dynamic_slice_in_dim(bias_parts, block * size, size, 1),
            ],
            axis=0,
        )
        if d:
            piece = lax.ppermute(piece, "pipe", [(i, (i + d) % sections) for i in range(sections)])
        pieces.append(piece)

    flat_cot = cotangent.reshape(rows * width, channels)
    own_cot = lax.dynamic_slice_in_dim(flat_cot, me * size, size, 1)
    grad_rows = pl.pallas_call(
        row_kernel,
        grid=(1,),
        in_specs=[
            pl.BlockSpec((count, 2 * rows * width), lambda i: (0, 0)),
            pl.BlockSpec((rows * width, size), lambda i: (0, 0)),
        ],
        out_specs=pl.BlockSpec((1, count, size), lambda i: (0, 0, 0)),
        out_shape=jax.ShapeDtypeStruct((1, count, size), BF16),
        name="cot_rows",
    )(forward_rows_doubled, own_cot)
    grad_columns = lax.all_to_all(
        grad_rows.reshape(columns, tile, size), "space", split_axis=0, concat_axis=0, tiled=True
    ).reshape(count, size)

    act_rows = pl.pallas_call(
        row_kernel,
        grid=(blocks,),
        in_specs=[
            pl.BlockSpec((count, 2 * rows * width), lambda i: (0, 0)),
            pl.BlockSpec((rows * width, size), lambda i: (0, i)),
        ],
        out_specs=pl.BlockSpec((1, count, size), lambda i: (i, 0, 0)),
        out_shape=jax.ShapeDtypeStruct((blocks, count, size), BF16),
        name="act_rows",
    )(forward_rows, activations.reshape(rows * width, channels))
    act_columns = lax.all_to_all(
        act_rows.reshape(blocks * columns, tile, size),
        ("pipe", "space"),
        split_axis=0,
        concat_axis=0,
        tiled=True,
    ).reshape(sections, count, size)

    vmem = pl.BlockSpec(memory_space=pltpu.VMEM)
    fold = lax.dynamic_slice_in_dim(jnp.asarray(folds), jnp.where(here == 0, 1, 0), 1, 0)
    back = pl.pallas_call(
        chain_kernel,
        in_specs=[pl.BlockSpec(memory_space=pltpu.SMEM)]
        + [vmem] * 5
        + [pl.BlockSpec(memory_space=pl.ANY)] * sections,
        out_specs=vmem,
        out_shape=jax.ShapeDtypeStruct((sections, count, size), BF16),
        scratch_shapes=[
            pltpu.VMEM((sections, 4 * size + 16, size), BF16),
            pltpu.SemaphoreType.DMA((sections,)),
        ],
        name="chain",
    )(
        me.reshape(1),
        act_columns,
        grad_columns,
        forward_columns,
        inverse_columns,
        fold,
        *pieces,
    )
    spec_rows = lax.all_to_all(
        back.reshape(sections * columns, tile, size),
        ("pipe", "space"),
        split_axis=0,
        concat_axis=0,
        tiled=True,
    ).reshape(blocks, count, size)
    grads = pl.pallas_call(
        inverse_kernel,
        grid=(blocks,),
        in_specs=[
            pl.BlockSpec((rows * width, 2 * count), lambda i: (0, 0)),
            pl.BlockSpec((1, count, size), lambda i: (i, 0, 0)),
            pl.BlockSpec((rows * width, size), lambda i: (0, i)),
        ],
        out_specs=pl.BlockSpec((rows * width, size), lambda i: (0, i)),
        out_shape=jax.ShapeDtypeStruct((rows * width, channels), BF16),
        name="inverse_rows",
    )(inverse_rows, spec_rows, flat_cot)
    return grads.reshape(1, rows, width, channels)


def solution(mesh):
    in_specs = (
        P("pipe", "space", None, None),
        P("space", None, None),
        P("pipe", None, None, None, None),
        P("pipe", None, None, None, None),
        P("pipe", None, None),
    )
    out_specs = P("pipe", "space", None, None)
    return jax.shard_map(body, mesh=mesh, in_specs=in_specs, out_specs=out_specs, check_vma=False)
```

```python
import math

import jax
import jax.numpy as jnp
import numpy as np
from jax import lax
from jax.experimental import pallas as pl
from jax.experimental.pallas import tpu as pltpu
from jax.sharding import PartitionSpec as P


BF16 = jnp.bfloat16
F32 = jnp.float32
X, Y, Z = 4, 4, 8


def two_parts(table):
    high = table.astype(np.float32).astype(BF16)
    low = (table - high.astype(np.float64)).astype(np.float32).astype(BF16)
    return np.concatenate([high, low], axis=1)


def row_matrix(rows, width, columns):
    modes = width // 2
    pair = modes // columns
    angles = 2.0 * math.pi * (np.outer(np.arange(modes), np.arange(width)) % width) / width
    scale = 1.0 / math.sqrt(width)
    parts = np.stack([np.cos(angles), -np.sin(angles)]) * scale
    table = np.zeros((columns, rows, 2, pair, rows, width))
    by_column = parts.reshape(2, columns, pair, width).transpose(1, 0, 2, 3)
    for h in range(rows):
        table[:, h, :, :, h, :] = by_column
    return table.reshape(columns * rows * 2 * pair, rows * width)


def column_matrix(height, pair):
    angles = 2.0 * math.pi * (np.outer(np.arange(height), np.arange(height)) % height) / height
    scale = 1.0 / math.sqrt(height)
    cosines, sines = np.cos(angles) * scale, np.sin(angles) * scale
    table = np.zeros((2, pair, height, height, 2, pair))
    for k in range(pair):
        table[0, k, :, :, 0, k] = cosines
        table[0, k, :, :, 1, k] = sines
        table[1, k, :, :, 1, k] = cosines
        table[1, k, :, :, 0, k] = -sines
    return table.reshape(2 * pair * height, 2 * pair * height)


def fold_matrices(height, pair):
    size = 2 * pair * height
    plain = np.eye(size)
    folded = np.eye(size).reshape(2, pair, height, 2, pair, height)
    eye = np.eye(height)
    flip = eye[(-np.arange(height)) % height]
    folded[0, 0, :, 0, 0, :] = 0.5 * (eye + flip)
    folded[1, 0, :, 1, 0, :] = 0.5 * (eye - flip)
    return np.stack([plain, folded.reshape(size, size)]).astype(np.float32).astype(BF16)


def dot(left, right):
    return jnp.dot(left, right, preferred_element_type=F32)


def dot_t(left, right):
    return lax.dot_general(left, right, (((1,), (1,)), ((), ())), preferred_element_type=F32)


def gelu_slope(values):
    return (
        0.5 * (1.0 + lax.erf(values * 0.7071067811865476))
        + values * jnp.exp(-0.5 * values * values) * 0.3989422804014327
    )


def twice(table_ref, operand):
    depth = operand.shape[0]
    return dot(table_ref[:, :depth], operand) + dot(table_ref[:, depth:], operand)


def place(where_ref):
    me, here = where_ref[0], where_ref[1]
    return lax.shift_right_logical(me, 1), me & 1, lax.shift_right_logical(here, 3), here & (Z - 1)


def prologue_kernel(where_ref, table_ref, act_ref, cot_ref, first_ref, second_ref, bias_ref, *rest):
    pieces, rows_ref, cots = rest[:Y], rest[Y], rest[Y + 1 : Y + 1 + Z]
    cot_buf, bias_buf, found, sems, cot_sem = rest[Y + 1 + Z :]
    size = cot_buf.shape[1] // 2
    y, c, x, z = place(where_ref)
    odd = x & 1
    cot_copy = pltpu.make_async_copy(cot_ref.at[:, pl.ds(y * 2 * size, 2 * size)], cot_buf, cot_sem)
    cot_copy.start()
    copies = []
    for d in range(Y):
        block = ((y + d) & (Y - 1)) * 2 + odd
        for i in range(2):
            for j, ref in enumerate((first_ref, second_ref)):
                copy = pltpu.make_async_copy(
                    ref.at[0, i, block],
                    pieces[d].at[pl.ds((2 * j + i) * size, size)],
                    sems.at[d, 2 * j + i],
                )
                copy.start()
                copies.append(copy)
        bias = bias_ref[0, :, pl.ds(block * size, size)]
        high = bias.astype(BF16).astype(F32)
        middle = (bias - high).astype(BF16).astype(F32)
        low = bias - high - middle
        packed = jnp.concatenate([high, middle, low, jnp.zeros((10, size), F32)], axis=0)
        bias_buf[d] = packed.astype(BF16)
        copy = pltpu.make_async_copy(bias_buf.at[d], pieces[d].at[pl.ds(4 * size, 16)], sems.at[d, 4])
        copy.start()
        copies.append(copy)

    depth = table_ref.shape[1] // 2
    half = table_ref.shape[0] // 2
    cot_copy.wait()
    own = pl.ds(pl.multiple_of(c * half, half), half)
    line = lax.broadcasted_iota(jnp.int32, (half, size), 0)
    zero_mode = jnp.logical_and(jnp.logical_and(line < 8, (line & 1) == 0), c == 0)
    factor = jnp.where(zero_mode, 1.0, 2.0).astype(F32)
    for k in range(2):
        field = cot_buf[:, k * size : (k + 1) * size]
        spectrum = dot(table_ref[own, :depth], field) + dot(table_ref[own, depth:], field)
        found[k] = (spectrum * factor).astype(BF16).reshape(half // 8, 8, size)
    for d in range(Z):
        to = (z + d) & (Z - 1)
        for k in range(X):
            cots[d][k] = found[k & 1, (k >> 1) * Z + to]

    for n in range(2 * Y):
        spectrum = twice(table_ref, act_ref[:, n * size : (n + 1) * size]).astype(BF16)
        rows_ref[n // 2, :, n % 2] = spectrum.reshape(4, half // 2, size)
    for copy in copies:
        copy.wait()


def turn_kernel(where_ref, *rest):
    arrived, outs = rest[:Z], rest[Z:]
    _, _, x, _ = place(where_ref)
    for e in range(X):
        to = (x + e) & (X - 1)
        for d in range(Z):
            outs[e][d] = arrived[d][to]


def inverse_kernel(table_ref, spec_ref, cot_ref, out_ref):
    rows = table_ref.shape[1] // 2
    size = spec_ref.shape[4]
    for k in range(2):
        block = slice(k * size, (k + 1) * size)
        field = twice(table_ref, spec_ref[0, :, k].reshape(rows, size))
        out_ref[:, block] = (field + cot_ref[:, block].astype(F32)).astype(BF16)


def chain_kernel(where_ref, act_ref, col_ref, inv_ref, fold_ref, *rest):
    sections = act_ref.shape[0]
    cots, weights = rest[:X], rest[X : X + sections]
    out_ref, held, found, sems = rest[X + sections :]
    size = act_ref.shape[2]
    half = act_ref.shape[1] // 2
    y, c, x, z = place(where_ref)
    copies = []
    for d in range(Y):
        for i in range(2):
            slot = ((y - d) & (Y - 1)) * 2 + (c if i == 0 else 1 - c)
            copy = pltpu.make_async_copy(weights[2 * d + i], held.at[slot], sems.at[2 * d + i])
            copy.start()
            copies.append(copy)
    for e in range(X):
        for d in range(Z):
            found[((x - e) & (X - 1)) * Z + ((z - d) & (Z - 1))] = cots[e][d]

    base = twice(col_ref, found[...].reshape(2 * half, size))
    total = jnp.zeros_like(base)
    height_total = jnp.zeros_like(base)
    grad = base.astype(BF16)
    spectra = [twice(col_ref, act_ref[p]).astype(BF16) for p in range(sections)]
    for copy in copies:
        copy.wait()

    for p in range(sections - 1, -1, -1):
        a_re, a_im = held[p, 0:size], held[p, size : 2 * size]
        b_re, b_im = held[p, 2 * size : 3 * size], held[p, 3 * size : 4 * size]
        bias = held[p, 4 * size : 4 * size + 16].astype(F32)
        bias_re = bias[0:1] + bias[2:3] + bias[4:5]
        bias_im = bias[1:2] + bias[3:4] + bias[5:6]
        s = spectra[p]
        s_turned = jnp.concatenate([-s[half:], s[:half]], axis=0)
        z_both = dot(s, a_re) + dot(s_turned, a_im)
        slope = gelu_slope(jnp.concatenate([z_both[:half] + bias_re, z_both[half:] + bias_im], axis=0))
        g_turned = jnp.concatenate([grad[half:], -grad[:half]], axis=0)
        u = dot_t(grad, b_re) + dot_t(g_turned, b_im)
        q = (u * slope).astype(BF16)
        q_turned = jnp.concatenate([q[half:], -q[:half]], axis=0)
        e = (dot_t(q, a_re) + dot_t(q_turned, a_im)).astype(BF16)
        height_total = height_total + twice(inv_ref, e)
        out_ref[p] = height_total.astype(BF16)
        if p > 0:
            total = total + dot(fold_ref[0], e)
            grad = (base + total).astype(BF16)


def body(activations, cotangent, w_first, w_second, b_first):
    sections = lax.axis_size("pipe")
    columns = lax.axis_size("space")
    me = lax.axis_index("pipe")
    here = lax.axis_index("space")
    _, rows, width, channels = activations.shape
    size = w_first.shape[3]
    height = rows * columns
    pair = width // 2 // columns
    count = rows * width
    tile = 2 * rows * pair
    forward_rows = two_parts(row_matrix(rows, width, columns))
    inverse_rows = two_parts(row_matrix(rows, width, columns).T)
    forward_columns = two_parts(column_matrix(height, pair))
    inverse_columns = two_parts(column_matrix(height, pair).T)
    folds = fold_matrices(height, pair)
    where = jnp.stack([me, here]).astype(jnp.int32)

    smem = pl.BlockSpec(memory_space=pltpu.SMEM)
    vmem = pl.BlockSpec(memory_space=pltpu.VMEM)
    hbm = pl.BlockSpec(memory_space=pl.ANY)

    def shaped(*dims):
        return jax.ShapeDtypeStruct(dims, BF16)

    def exchange(value):
        return lax.all_to_all(
            value.reshape(sections * columns, tile, size),
            ("pipe", "space"),
            split_axis=0,
            concat_axis=0,
            tiled=True,
        )

    flat_cot = cotangent.reshape(count, channels)
    made = pl.pallas_call(
        prologue_kernel,
        in_specs=[smem, vmem, vmem, hbm, hbm, hbm, vmem],
        out_specs=[hbm] * Y + [vmem] * (1 + Z),
        out_shape=[shaped(4 * size + 16, size)] * Y
        + [shaped(Y, 4, 2, count // 4, size)]
        + [shaped(X, tile, size)] * Z,
        scratch_shapes=[
            pltpu.VMEM((count, 2 * size), BF16),
            pltpu.VMEM((Y, 16, size), BF16),
            pltpu.VMEM((2, columns // 2, tile, size), BF16),
            pltpu.SemaphoreType.DMA((Y, 5)),
            pltpu.SemaphoreType.DMA(()),
        ],
        name="prologue",
    )(where, forward_rows, activations.reshape(count, channels), flat_cot, w_first, w_second, b_first)
    pieces, act_rows, cot_rows = made[:Y], made[Y], made[Y + 1 :]

    weights = []
    for d in range(Y):
        route = [(i, (i + 2 * d) % sections) for i in range(sections)]
        piece = lax.ppermute(pieces[d], "pipe", route) if d else pieces[0]
        weights += [piece, lax.ppermute(piece, "pipe", [(i, i ^ 1) for i in range(sections)])]

    arrived = [cot_rows[0]]
    for d in range(1, Z):
        route = [(x * Z + z, x * Z + (z + d) % Z) for x in range(X) for z in range(Z)]
        arrived.append(lax.ppermute(cot_rows[d], "space", route))
    turned = pl.pallas_call(
        turn_kernel,
        in_specs=[smem] + [vmem] * Z,
        out_specs=[vmem] * X,
        out_shape=[shaped(Z, tile, size)] * X,
        name="turn",
    )(where, *arrived)
    cots = [turned[0]]
    for e in range(1, X):
        route = [(x * Z + z, (x + e) % X * Z + z) for x in range(X) for z in range(Z)]
        cots.append(lax.ppermute(turned[e], "space", route))

    act_columns = exchange(act_rows).reshape(sections, count, size)

    y, core, x, z = lax.div(me, 2), lax.rem(me, 2), lax.div(here, Z), lax.rem(here, Z)
    has_zero = jnp.logical_and(jnp.logical_and(core == 0, x < 2), z == 0)
    fold = lax.dynamic_slice_in_dim(jnp.asarray(folds), jnp.where(has_zero, 1, 0), 1, 0)
    back = pl.pallas_call(
        chain_kernel,
        in_specs=[smem] + [vmem] * (4 + X) + [hbm] * sections,
        out_specs=vmem,
        out_shape=shaped(sections, count, size),
        scratch_shapes=[
            pltpu.VMEM((sections, 4 * size + 16, size), BF16),
            pltpu.VMEM((columns, tile, size), BF16),
            pltpu.SemaphoreType.DMA((sections,)),
        ],
        name="chain",
    )(where, act_columns, forward_columns, inverse_columns, fold, *cots, *weights)
    spec_rows = exchange(back).reshape(Y, 4, 2, count // 4, size)
    grads = pl.pallas_call(
        inverse_kernel,
        grid=(Y,),
        in_specs=[
            pl.BlockSpec((count, 2 * count), lambda i: (0, 0)),
            pl.BlockSpec((1, 4, 2, count // 4, size), lambda i: (i, 0, 0, 0, 0)),
            pl.BlockSpec((count, 2 * size), lambda i: (0, i)),
        ],
        out_specs=pl.BlockSpec((count, 2 * size), lambda i: (0, i)),
        out_shape=shaped(count, channels),
        name="inverse_rows",
    )(inverse_rows, spec_rows, flat_cot)
    return grads.reshape(1, rows, width, channels)


def solution(mesh):
    in_specs = (
        P("pipe", "space", None, None),
        P("space", None, None),
        P("pipe", None, None, None, None),
        P("pipe", None, None, None, None),
        P("pipe", None, None),
    )
    out_specs = P("pipe", "space", None, None)
    return jax.shard_map(body, mesh=mesh, in_specs=in_specs, out_specs=out_specs, check_vma=False)
```

```python
import math

import jax
import jax.numpy as jnp
import numpy as np
from jax import lax
from jax.experimental import pallas as pl
from jax.experimental.pallas import tpu as pltpu
from jax.sharding import Mesh
from jax.sharding import PartitionSpec as P


BF16 = jnp.bfloat16
F32 = jnp.float32
X, Y, Z = 4, 4, 8
EVERYONE = ("z", "core", "x", "y")


def two_parts(table):
    high = table.astype(np.float32).astype(BF16)
    low = (table - high.astype(np.float64)).astype(np.float32).astype(BF16)
    return np.concatenate([high, low], axis=1)


def row_matrix(rows, width, columns):
    modes = width // 2
    pair = modes // columns
    angles = 2.0 * math.pi * (np.outer(np.arange(modes), np.arange(width)) % width) / width
    scale = 1.0 / math.sqrt(width)
    parts = np.stack([np.cos(angles), -np.sin(angles)]) * scale
    table = np.zeros((columns, rows, 2, pair, rows, width))
    by_column = parts.reshape(2, columns, pair, width).transpose(1, 0, 2, 3)
    for h in range(rows):
        table[:, h, :, :, h, :] = by_column
    return table.reshape(columns * rows * 2 * pair, rows * width)


def column_matrix(height, pair):
    angles = 2.0 * math.pi * (np.outer(np.arange(height), np.arange(height)) % height) / height
    scale = 1.0 / math.sqrt(height)
    cosines, sines = np.cos(angles) * scale, np.sin(angles) * scale
    table = np.zeros((2, pair, height, height, 2, pair))
    for k in range(pair):
        table[0, k, :, :, 0, k] = cosines
        table[0, k, :, :, 1, k] = sines
        table[1, k, :, :, 1, k] = cosines
        table[1, k, :, :, 0, k] = -sines
    return table.reshape(2 * pair * height, 2 * pair * height)


def fold_matrices(height, pair):
    size = 2 * pair * height
    plain = np.eye(size)
    folded = np.eye(size).reshape(2, pair, height, 2, pair, height)
    eye = np.eye(height)
    flip = eye[(-np.arange(height)) % height]
    folded[0, 0, :, 0, 0, :] = 0.5 * (eye + flip)
    folded[1, 0, :, 1, 0, :] = 0.5 * (eye - flip)
    return np.stack([plain, folded.reshape(size, size)]).astype(np.float32).astype(BF16)


def dot(left, right):
    return jnp.dot(left, right, preferred_element_type=F32)


def dot_t(left, right):
    return lax.dot_general(left, right, (((1,), (1,)), ((), ())), preferred_element_type=F32)


def gelu_slope(values):
    return (
        0.5 * (1.0 + lax.erf(values * 0.7071067811865476))
        + values * jnp.exp(-0.5 * values * values) * 0.3989422804014327
    )


def twice(table_ref, operand):
    depth = operand.shape[0]
    return dot(table_ref[:, :depth], operand) + dot(table_ref[:, depth:], operand)


def prologue_kernel(table_ref, act_ref, cot_ref, first_ref, second_ref, bias_ref, *rest):
    pieces, rows_ref, cots = rest[:Y], rest[Y], rest[Y + 1 : Y + 1 + Z]
    cot_buf, held, found, sems, cot_sem = rest[Y + 1 + Z :]
    size = cot_buf.shape[1] // 2
    y, core, x, z = (lax.axis_index(name) for name in ("y", "core", "x", "z"))
    odd = x & 1
    cot_copy = pltpu.make_async_copy(cot_ref.at[:, pl.ds(y * 2 * size, 2 * size)], cot_buf, cot_sem)
    cot_copy.start()
    loads = []
    for d in range(Y):
        block = ((y + d) & (Y - 1)) * 2 + odd
        for i in range(2):
            for j, ref in enumerate((first_ref, second_ref)):
                copy = pltpu.make_async_copy(
                    ref.at[0, i, block],
                    held.at[d, pl.ds((2 * j + i) * size, size)],
                    sems.at[d, 2 * j + i],
                )
                copy.start()
                loads.append(copy)

    count = table_ref.shape[0]
    line = lax.broadcasted_iota(jnp.int32, (count, size), 0)
    factor = jnp.where(jnp.logical_and(line < 8, (line & 1) == 0), 1.0, 2.0).astype(F32)
    cot_copy.wait()
    for k in range(2):
        spectrum = (twice(table_ref, cot_buf[:, k * size : (k + 1) * size]) * factor).astype(BF16)
        found[k] = spectrum.reshape(Z, 2, 2, 8, size)
    for d in range(Z):
        to = (z + d) & (Z - 1)
        for k in range(X):
            cots[d][k] = found[k & 1, to, core, k >> 1]

    for d in range(Y):
        block = ((y + d) & (Y - 1)) * 2 + odd
        bias = bias_ref[0, :, pl.ds(block * size, size)]
        high = bias.astype(BF16).astype(F32)
        middle = (bias - high).astype(BF16).astype(F32)
        low = bias - high - middle
        packed = jnp.concatenate([high, middle, low, jnp.zeros((10, size), F32)], axis=0)
        held[d, 4 * size : 4 * size + 16] = packed.astype(BF16)
    for copy in loads:
        copy.wait()
    stores = []
    for d in range(Y):
        copy = pltpu.make_async_copy(held.at[d], pieces[d], sems.at[d, 4])
        copy.start()
        stores.append(copy)

    for n in range(2 * Y):
        spectrum = twice(table_ref, act_ref[:, n * size : (n + 1) * size]).astype(BF16)
        rows_ref[:, :, :, n % 2, n // 2] = spectrum.reshape(Z, 2, 2, 8, size)
    for copy in stores:
        copy.wait()


def turn_kernel(*refs):
    arrived, outs = refs[:Z], refs[Z:]
    x = lax.axis_index("x")
    for e in range(X):
        to = (x + e) & (X - 1)
        for d in range(Z):
            outs[e][d] = arrived[d][to]


def inverse_kernel(table_ref, spec_ref, cot_ref, out_ref, result, sems):
    rows = table_ref.shape[0]
    size = spec_ref.shape[6]
    copies = []
    for n in range(2 * Y):
        block = slice(n * size, (n + 1) * size)
        field = twice(table_ref, spec_ref[:, :, :, n % 2, n // 2].reshape(rows, size))
        result[:, block] = (field + cot_ref[:, block].astype(F32)).astype(BF16)
        copy = pltpu.make_async_copy(result.at[:, block], out_ref.at[:, block], sems.at[n])
        copy.start()
        copies.append(copy)
    for copy in copies:
        copy.wait()


def chain_kernel(act_ref, col_ref, inv_ref, fold_ref, *rest):
    sections = 2 * Y
    cots, weights = rest[:X], rest[X : X + sections]
    out_ref, held, found, sems = rest[X + sections :]
    size = act_ref.shape[6]
    half = col_ref.shape[0] // 2
    y, core, x, z = (lax.axis_index(name) for name in ("y", "core", "x", "z"))
    copies = []
    for d in range(Y):
        for i in range(2):
            slot = ((y - d) & (Y - 1)) * 2 + (core if i == 0 else 1 - core)
            copy = pltpu.make_async_copy(weights[2 * d + i], held.at[slot], sems.at[2 * d + i])
            copy.start()
            copies.append(copy)
    for e in range(X):
        for d in range(Z):
            found[(z - d) & (Z - 1), (x - e) & (X - 1)] = cots[e][d]
    has_zero = jnp.logical_and(jnp.logical_and(core == 0, x < 2), z == 0)
    fold = jnp.where(has_zero, 1, 0)

    base = twice(col_ref, found[...].reshape(2 * half, size))
    total = jnp.zeros_like(base)
    height_total = jnp.zeros_like(base)
    grad = base.astype(BF16)
    spectra = []
    for p in range(sections):
        columns = act_ref[:, p % 2, :, :, p // 2].reshape(2 * half, size)
        spectra.append(twice(col_ref, columns).astype(BF16))
    for copy in copies:
        copy.wait()

    for p in range(sections - 1, -1, -1):
        a_re, a_im = held[p, 0:size], held[p, size : 2 * size]
        b_re, b_im = held[p, 2 * size : 3 * size], held[p, 3 * size : 4 * size]
        bias = held[p, 4 * size : 4 * size + 16].astype(F32)
        bias_re = bias[0:1] + bias[2:3] + bias[4:5]
        bias_im = bias[1:2] + bias[3:4] + bias[5:6]
        s = spectra[p]
        s_turned = jnp.concatenate([-s[half:], s[:half]], axis=0)
        z_both = dot(s, a_re) + dot(s_turned, a_im)
        slope = gelu_slope(jnp.concatenate([z_both[:half] + bias_re, z_both[half:] + bias_im], axis=0))
        g_turned = jnp.concatenate([grad[half:], -grad[:half]], axis=0)
        u = dot_t(grad, b_re) + dot_t(g_turned, b_im)
        q = (u * slope).astype(BF16)
        q_turned = jnp.concatenate([q[half:], -q[:half]], axis=0)
        e = (dot_t(q, a_re) + dot_t(q_turned, a_im)).astype(BF16)
        height_total = height_total + twice(inv_ref, e)
        out_ref[:, p % 2, :, :, p // 2] = height_total.astype(BF16).reshape(Z, 2, 2, 8, size)
        if p > 0:
            total = total + dot(fold_ref[fold], e)
            grad = (base + total).astype(BF16)


def body(activations, cotangent, w_first, w_second, b_first):
    sections, columns = 2 * Y, X * Z
    _, rows, width, channels = activations.shape
    size = w_first.shape[3]
    height = rows * columns
    pair = width // 2 // columns
    count = rows * width
    tile = 2 * rows * pair
    row_table = row_matrix(rows, width, columns)
    row_table = row_table.reshape(2, 2, Z, -1).transpose(2, 0, 1, 3).reshape(row_table.shape)
    forward_rows, inverse_rows = two_parts(row_table), two_parts(row_table.T)
    column_table = column_matrix(height, pair)
    column_table = column_table.reshape(-1, X, Z, tile).transpose(0, 2, 1, 3).reshape(column_table.shape)
    forward_columns, inverse_columns = two_parts(column_table), two_parts(column_table.T)
    folds = fold_matrices(height, pair)

    vmem = pl.BlockSpec(memory_space=pltpu.VMEM)
    hbm = pl.BlockSpec(memory_space=pl.ANY)
    blocks = (Z, 2, 2, 2, Y, tile, size)

    def shaped(*dims):
        return jax.ShapeDtypeStruct(dims, BF16)

    def exchange(value):
        flat = value.reshape(sections * columns, tile, size)
        return lax.all_to_all(flat, EVERYONE, split_axis=0, concat_axis=0, tiled=True).reshape(blocks)

    def shifted(value, axis, distance):
        size = lax.axis_size(axis)
        return lax.ppermute(value, axis, [(i, (i + distance) % size) for i in range(size)])

    flat_cot = cotangent.reshape(count, channels)
    made = pl.pallas_call(
        prologue_kernel,
        in_specs=[vmem, vmem, hbm, hbm, hbm, vmem],
        out_specs=[hbm] * Y + [vmem] * (1 + Z),
        out_shape=[shaped(4 * size + 16, size)] * Y + [shaped(*blocks)] + [shaped(X, tile, size)] * Z,
        scratch_shapes=[
            pltpu.VMEM((count, 2 * size), BF16),
            pltpu.VMEM((Y, 4 * size + 16, size), BF16),
            pltpu.VMEM((2, Z, 2, 2, tile, size), BF16),
            pltpu.SemaphoreType.DMA((Y, 5)),
            pltpu.SemaphoreType.DMA(()),
        ],
        name="prologue",
    )(forward_rows, activations.reshape(count, channels), flat_cot, w_first, w_second, b_first)
    pieces, act_rows, cot_rows = made[:Y], made[Y], made[Y + 1 :]

    arrived = [cot_rows[0]]
    arrived += [shifted(cot_rows[d], "z", d) for d in range(1, Z)]
    weights = []
    for d in range(Y):
        piece = shifted(pieces[d], "y", d) if d else pieces[0]
        weights += [piece, shifted(piece, "core", 1)]
    act_columns = exchange(act_rows)
    turned = pl.pallas_call(
        turn_kernel,
        in_specs=[vmem] * Z,
        out_specs=[vmem] * X,
        out_shape=[shaped(Z, tile, size)] * X,
        name="turn",
    )(*arrived)
    cots = [turned[0]] + [shifted(turned[e], "x", e) for e in range(1, X)]

    back = pl.pallas_call(
        chain_kernel,
        in_specs=[vmem] * (4 + X) + [hbm] * sections,
        out_specs=vmem,
        out_shape=shaped(*blocks),
        scratch_shapes=[
            pltpu.VMEM((sections, 4 * size + 16, size), BF16),
            pltpu.VMEM((Z, X, tile, size), BF16),
            pltpu.SemaphoreType.DMA((sections,)),
        ],
        name="chain",
    )(act_columns, forward_columns, inverse_columns, folds, *cots, *weights)
    grads = pl.pallas_call(
        inverse_kernel,
        in_specs=[vmem] * 3,
        out_specs=hbm,
        out_shape=shaped(count, channels),
        scratch_shapes=[pltpu.VMEM((count, channels), BF16), pltpu.SemaphoreType.DMA((sections,))],
        name="inverse_rows",
    )(inverse_rows, exchange(back), flat_cot)
    return grads.reshape(1, rows, width, channels)


def solution(mesh):
    chips = Mesh(mesh.devices.reshape(Y, 2, X, Z), ("y", "core", "x", "z"))
    pipe, space = ("y", "core"), ("x", "z")
    in_specs = (
        P(pipe, space, None, None),
        P(space, None, None),
        P(pipe, None, None, None, None),
        P(pipe, None, None, None, None),
        P(pipe, None, None),
    )
    out_specs = P(pipe, space, None, None)
    return jax.shard_map(body, mesh=chips, in_specs=in_specs, out_specs=out_specs, check_vma=False)
```

```python
import math

import jax
import jax.numpy as jnp
import numpy as np
from jax import lax
from jax.experimental import pallas as pl
from jax.experimental.pallas import tpu as pltpu
from jax.sharding import Mesh
from jax.sharding import PartitionSpec as P


BF16 = jnp.bfloat16
F32 = jnp.float32
X, Y, Z = 4, 4, 8
EVERYONE = ("z", "core", "x", "y")


def two_parts(table):
    high = table.astype(np.float32).astype(BF16)
    low = (table - high.astype(np.float64)).astype(np.float32).astype(BF16)
    return np.concatenate([high, low], axis=1)


def row_matrix(rows, width, columns):
    modes = width // 2
    pair = modes // columns
    angles = 2.0 * math.pi * (np.outer(np.arange(modes), np.arange(width)) % width) / width
    scale = 1.0 / math.sqrt(width)
    parts = np.stack([np.cos(angles), -np.sin(angles)]) * scale
    table = np.zeros((columns, rows, 2, pair, rows, width))
    by_column = parts.reshape(2, columns, pair, width).transpose(1, 0, 2, 3)
    for h in range(rows):
        table[:, h, :, :, h, :] = by_column
    return table.reshape(columns * rows * 2 * pair, rows * width)


def column_matrix(height, pair):
    angles = 2.0 * math.pi * (np.outer(np.arange(height), np.arange(height)) % height) / height
    scale = 1.0 / math.sqrt(height)
    cosines, sines = np.cos(angles) * scale, np.sin(angles) * scale
    table = np.zeros((2, pair, height, height, 2, pair))
    for k in range(pair):
        table[0, k, :, :, 0, k] = cosines
        table[0, k, :, :, 1, k] = sines
        table[1, k, :, :, 1, k] = cosines
        table[1, k, :, :, 0, k] = -sines
    return table.reshape(2 * pair * height, 2 * pair * height)


def fold_matrices(height, pair):
    size = 2 * pair * height
    plain = np.eye(size)
    folded = np.eye(size).reshape(2, pair, height, 2, pair, height)
    eye = np.eye(height)
    flip = eye[(-np.arange(height)) % height]
    folded[0, 0, :, 0, 0, :] = 0.5 * (eye + flip)
    folded[1, 0, :, 1, 0, :] = 0.5 * (eye - flip)
    return np.stack([plain, folded.reshape(size, size)]).astype(np.float32).astype(BF16)


def dot(left, right):
    return jnp.dot(left, right, preferred_element_type=F32)


def dot_t(left, right):
    return lax.dot_general(left, right, (((1,), (1,)), ((), ())), preferred_element_type=F32)


def gelu_slope(values):
    return (
        0.5 * (1.0 + lax.erf(values * 0.7071067811865476))
        + values * jnp.exp(-0.5 * values * values) * 0.3989422804014327
    )


def twice(table_ref, operand):
    depth = operand.shape[0]
    return dot(table_ref[:, :depth], operand) + dot(table_ref[:, depth:], operand)


def cot_kernel(table_ref, cot_ref, out_ref, table, field, sems):
    size = out_ref.shape[3]
    depth = table.shape[2] // 2
    y, core = lax.axis_index("y"), lax.axis_index("core")
    copies = [
        pltpu.make_async_copy(table_ref.at[:, core], table, sems.at[0]),
        pltpu.make_async_copy(cot_ref.at[:, pl.ds(y * 2 * size, 2 * size)], field, sems.at[1]),
    ]
    for copy in copies:
        copy.start()
    half = Z * table.shape[1]
    line = lax.broadcasted_iota(jnp.int32, (half, size), 0)
    zero_mode = jnp.logical_and(jnp.logical_and(line < 8, (line & 1) == 0), core == 0)
    factor = jnp.where(zero_mode, 1.0, 2.0).astype(F32)
    for copy in copies:
        copy.wait()
    high = table[:, :, :depth].reshape(half, depth)
    low = table[:, :, depth:].reshape(half, depth)
    for k in range(2):
        part = field[:, k * size : (k + 1) * size]
        spectrum = ((dot(high, part) + dot(low, part)) * factor).astype(BF16).reshape(Z, 2, 8, size)
        for m in range(2):
            out_ref[:, 2 * m + k] = spectrum[:, m]


def prologue_kernel(table_ref, act_ref, first_ref, second_ref, bias_ref, *rest):
    pieces = rest[:Y]
    rows_ref, held, sems = rest[Y:]
    size = held.shape[2]
    y, odd = lax.axis_index("y"), lax.axis_index("x") & 1
    loads = []
    for d in range(Y):
        block = ((y + d) & (Y - 1)) * 2 + odd
        for i in range(2):
            for j, ref in enumerate((first_ref, second_ref)):
                copy = pltpu.make_async_copy(
                    ref.at[0, i, block],
                    held.at[d, pl.ds((2 * j + i) * size, size)],
                    sems.at[d, 2 * j + i],
                )
                copy.start()
                loads.append(copy)
        bias = bias_ref[0, :, pl.ds(block * size, size)]
        high = bias.astype(BF16).astype(F32)
        middle = (bias - high).astype(BF16).astype(F32)
        low = bias - high - middle
        packed = jnp.concatenate([high, middle, low, jnp.zeros((10, size), F32)], axis=0)
        held[d, 4 * size : 4 * size + 16] = packed.astype(BF16)

    stores = []
    for n in range(2 * Y):
        if n == 2:
            for copy in loads:
                copy.wait()
            for d in range(Y):
                copy = pltpu.make_async_copy(held.at[d], pieces[d], sems.at[d, 4])
                copy.start()
                stores.append(copy)
        spectrum = twice(table_ref, act_ref[:, n * size : (n + 1) * size]).astype(BF16)
        rows_ref[:, :, :, n % 2, n // 2] = spectrum.reshape(Z, 2, 2, 8, size)
    for copy in stores:
        copy.wait()


def turn_kernel(arrived_ref, *outs):
    x = lax.axis_index("x")
    for e in range(X):
        outs[e][...] = arrived_ref[:, (x + e) & (X - 1)]


def inverse_kernel(table_ref, spec_ref, cot_ref, out_ref, result, sems):
    rows = table_ref.shape[0]
    size = spec_ref.shape[6]
    copies = []
    for n in range(2 * Y):
        block = slice(n * size, (n + 1) * size)
        field = twice(table_ref, spec_ref[:, :, :, n % 2, n // 2].reshape(rows, size))
        result[:, block] = (field + cot_ref[:, block].astype(F32)).astype(BF16)
        copy = pltpu.make_async_copy(result.at[:, block], out_ref.at[:, block], sems.at[n])
        copy.start()
        copies.append(copy)
    for copy in copies:
        copy.wait()


def chain_kernel(act_ref, col_ref, inv_ref, fold_ref, *rest):
    sections = 2 * Y
    cots, weights = rest[:X], rest[X : X + sections]
    out_ref, held, found, sems = rest[X + sections :]
    size = act_ref.shape[6]
    half = col_ref.shape[0] // 2
    y, core, x, z = (lax.axis_index(name) for name in ("y", "core", "x", "z"))
    copies = []
    for d in range(Y):
        for i in range(2):
            slot = ((y - d) & (Y - 1)) * 2 + (core if i == 0 else 1 - core)
            copy = pltpu.make_async_copy(weights[2 * d + i], held.at[slot], sems.at[2 * d + i])
            copy.start()
            copies.append(copy)
    for e in range(X):
        found[:, (x - e) & (X - 1)] = cots[e][...]
    has_zero = jnp.logical_and(jnp.logical_and(core == 0, x < 2), z == 0)
    fold = jnp.where(has_zero, 1, 0)

    base = twice(col_ref, found[...].reshape(2 * half, size))
    total = jnp.zeros_like(base)
    height_total = jnp.zeros_like(base)
    grad = base.astype(BF16)
    spectra = []
    for p in range(sections):
        columns = act_ref[:, p % 2, :, :, p // 2].reshape(2 * half, size)
        spectra.append(twice(col_ref, columns).astype(BF16))
    for copy in copies:
        copy.wait()

    for p in range(sections - 1, -1, -1):
        a_re, a_im = held[p, 0:size], held[p, size : 2 * size]
        b_re, b_im = held[p, 2 * size : 3 * size], held[p, 3 * size : 4 * size]
        bias = held[p, 4 * size : 4 * size + 16].astype(F32)
        bias_re = bias[0:1] + bias[2:3] + bias[4:5]
        bias_im = bias[1:2] + bias[3:4] + bias[5:6]
        s = spectra[p]
        s_turned = jnp.concatenate([-s[half:], s[:half]], axis=0)
        z_both = dot(s, a_re) + dot(s_turned, a_im)
        slope = gelu_slope(jnp.concatenate([z_both[:half] + bias_re, z_both[half:] + bias_im], axis=0))
        g_turned = jnp.concatenate([grad[half:], -grad[:half]], axis=0)
        u = dot_t(grad, b_re) + dot_t(g_turned, b_im)
        q = (u * slope).astype(BF16)
        q_turned = jnp.concatenate([q[half:], -q[:half]], axis=0)
        e = (dot_t(q, a_re) + dot_t(q_turned, a_im)).astype(BF16)
        height_total = height_total + twice(inv_ref, e)
        out_ref[:, p % 2, :, :, p // 2] = height_total.astype(BF16).reshape(Z, 2, 2, 8, size)
        if p > 0:
            total = total + dot(fold_ref[fold], e)
            grad = (base + total).astype(BF16)


def body(activations, cotangent, w_first, w_second, b_first):
    sections, columns = 2 * Y, X * Z
    _, rows, width, channels = activations.shape
    size = w_first.shape[3]
    height = rows * columns
    pair = width // 2 // columns
    count = rows * width
    tile = 2 * rows * pair
    row_table = row_matrix(rows, width, columns)
    row_table = row_table.reshape(2, 2, Z, -1).transpose(2, 0, 1, 3).reshape(row_table.shape)
    forward_rows, inverse_rows = two_parts(row_table), two_parts(row_table.T)
    column_table = column_matrix(height, pair)
    column_table = column_table.reshape(-1, X, Z, tile).transpose(0, 2, 1, 3).reshape(column_table.shape)
    forward_columns, inverse_columns = two_parts(column_table), two_parts(column_table.T)
    folds = fold_matrices(height, pair)

    vmem = pl.BlockSpec(memory_space=pltpu.VMEM)
    hbm = pl.BlockSpec(memory_space=pl.ANY)
    blocks = (Z, 2, 2, 2, Y, tile, size)

    def shaped(*dims):
        return jax.ShapeDtypeStruct(dims, BF16)

    def exchange(value):
        flat = value.reshape(sections * columns, tile, size)
        return lax.all_to_all(flat, EVERYONE, split_axis=0, concat_axis=0, tiled=True).reshape(blocks)

    def shifted(value, axis, distance):
        size = lax.axis_size(axis)
        return lax.ppermute(value, axis, [(i, (i + distance) % size) for i in range(size)])

    flat_cot = cotangent.reshape(count, channels)
    cot_rows = pl.pallas_call(
        cot_kernel,
        in_specs=[hbm, hbm],
        out_specs=vmem,
        out_shape=shaped(Z, X, tile, size),
        scratch_shapes=[
            pltpu.VMEM((Z, 2 * tile, 2 * count), BF16),
            pltpu.VMEM((count, 2 * size), BF16),
            pltpu.SemaphoreType.DMA((2,)),
        ],
        name="cot_rows",
    )(forward_rows.reshape(Z, 2, 2 * tile, 2 * count), flat_cot)
    cot_blocks = lax.all_to_all(
        cot_rows.reshape(Z, X * tile, size), "z", split_axis=0, concat_axis=0, tiled=True
    ).reshape(cot_rows.shape)
    made = pl.pallas_call(
        prologue_kernel,
        in_specs=[vmem, vmem, hbm, hbm, vmem],
        out_specs=[hbm] * Y + [vmem],
        out_shape=[shaped(4 * size + 16, size)] * Y + [shaped(*blocks)],
        scratch_shapes=[
            pltpu.VMEM((Y, 4 * size + 16, size), BF16),
            pltpu.SemaphoreType.DMA((Y, 5)),
        ],
        name="prologue",
    )(forward_rows, activations.reshape(count, channels), w_first, w_second, b_first)
    pieces, act_rows = made[:Y], made[Y]

    weights = []
    for d in range(Y):
        piece = shifted(pieces[d], "y", d) if d else pieces[0]
        weights += [piece, shifted(piece, "core", 1)]
    act_columns = exchange(act_rows)
    turned = pl.pallas_call(
        turn_kernel,
        in_specs=[vmem],
        out_specs=[vmem] * X,
        out_shape=[shaped(Z, tile, size)] * X,
        name="turn",
    )(cot_blocks)
    cots = [turned[0]] + [shifted(turned[e], "x", e) for e in range(1, X)]

    back = pl.pallas_call(
        chain_kernel,
        in_specs=[vmem] * (4 + X) + [hbm] * sections,
        out_specs=vmem,
        out_shape=shaped(*blocks),
        scratch_shapes=[
            pltpu.VMEM((sections, 4 * size + 16, size), BF16),
            pltpu.VMEM((Z, X, tile, size), BF16),
            pltpu.SemaphoreType.DMA((sections,)),
        ],
        name="chain",
    )(act_columns, forward_columns, inverse_columns, folds, *cots, *weights)
    grads = pl.pallas_call(
        inverse_kernel,
        in_specs=[vmem] * 3,
        out_specs=hbm,
        out_shape=shaped(count, channels),
        scratch_shapes=[pltpu.VMEM((count, channels), BF16), pltpu.SemaphoreType.DMA((sections,))],
        name="inverse_rows",
    )(inverse_rows, exchange(back), flat_cot)
    return grads.reshape(1, rows, width, channels)


def solution(mesh):
    chips = Mesh(mesh.devices.reshape(Y, 2, X, Z), ("y", "core", "x", "z"))
    pipe, space = ("y", "core"), ("x", "z")
    in_specs = (
        P(pipe, space, None, None),
        P(space, None, None),
        P(pipe, None, None, None, None),
        P(pipe, None, None, None, None),
        P(pipe, None, None),
    )
    out_specs = P(pipe, space, None, None)
    return jax.shard_map(body, mesh=chips, in_specs=in_specs, out_specs=out_specs, check_vma=False)
```

```python
import math

import jax
import jax.numpy as jnp
import numpy as np
from jax import lax
from jax.experimental import pallas as pl
from jax.experimental.pallas import tpu as pltpu
from jax.sharding import Mesh
from jax.sharding import PartitionSpec as P


BF16 = jnp.bfloat16
F32 = jnp.float32
X, Y, Z = 4, 4, 8
SMALL = pltpu.CompilerParams(vmem_limit_bytes=20 << 20)
EVERYONE = ("z", "core", "x", "y")


def two_parts(table):
    high = table.astype(np.float32).astype(BF16)
    low = (table - high.astype(np.float64)).astype(np.float32).astype(BF16)
    return np.concatenate([high, low], axis=1)


def row_matrix(rows, width, columns):
    modes = width // 2
    pair = modes // columns
    angles = 2.0 * math.pi * (np.outer(np.arange(modes), np.arange(width)) % width) / width
    scale = 1.0 / math.sqrt(width)
    parts = np.stack([np.cos(angles), -np.sin(angles)]) * scale
    table = np.zeros((columns, rows, 2, pair, rows, width))
    by_column = parts.reshape(2, columns, pair, width).transpose(1, 0, 2, 3)
    for h in range(rows):
        table[:, h, :, :, h, :] = by_column
    return table.reshape(columns * rows * 2 * pair, rows * width)


def column_matrix(height, pair):
    angles = 2.0 * math.pi * (np.outer(np.arange(height), np.arange(height)) % height) / height
    scale = 1.0 / math.sqrt(height)
    cosines, sines = np.cos(angles) * scale, np.sin(angles) * scale
    table = np.zeros((2, pair, height, height, 2, pair))
    for k in range(pair):
        table[0, k, :, :, 0, k] = cosines
        table[0, k, :, :, 1, k] = sines
        table[1, k, :, :, 1, k] = cosines
        table[1, k, :, :, 0, k] = -sines
    return table.reshape(2 * pair * height, 2 * pair * height)


def fold_matrices(height, pair):
    size = 2 * pair * height
    plain = np.eye(size)
    folded = np.eye(size).reshape(2, pair, height, 2, pair, height)
    eye = np.eye(height)
    flip = eye[(-np.arange(height)) % height]
    folded[0, 0, :, 0, 0, :] = 0.5 * (eye + flip)
    folded[1, 0, :, 1, 0, :] = 0.5 * (eye - flip)
    return np.stack([plain, folded.reshape(size, size)]).astype(np.float32).astype(BF16)


def dot(left, right):
    return jnp.dot(left, right, preferred_element_type=F32)


def dot_t(left, right):
    return lax.dot_general(left, right, (((1,), (1,)), ((), ())), preferred_element_type=F32)


def gelu_slope(values):
    return (
        0.5 * (1.0 + lax.erf(values * 0.7071067811865476))
        + values * jnp.exp(-0.5 * values * values) * 0.3989422804014327
    )


def twice(table_ref, operand):
    depth = operand.shape[0]
    return dot(table_ref[:, :depth], operand) + dot(table_ref[:, depth:], operand)


def first_kernel(table_ref, cot_ref, first_ref, second_ref, bias_ref, *rest):
    pieces = rest[:Y]
    out_ref, table, field, sems, cot_sems = rest[Y:]
    size = out_ref.shape[3]
    depth = table.shape[2] // 2
    y, core, odd = lax.axis_index("y"), lax.axis_index("core"), lax.axis_index("x") & 1
    copies = [
        pltpu.make_async_copy(table_ref.at[:, core], table, cot_sems.at[0]),
        pltpu.make_async_copy(cot_ref.at[:, pl.ds(y * 2 * size, 2 * size)], field, cot_sems.at[1]),
    ]
    for copy in copies:
        copy.start()
    loads = []
    for d in range(Y):
        block = ((y + d) & (Y - 1)) * 2 + odd
        for i in range(2):
            for j, ref in enumerate((first_ref, second_ref)):
                copy = pltpu.make_async_copy(
                    ref.at[0, i, block],
                    pieces[d].at[pl.ds((2 * j + i) * size, size)],
                    sems.at[d, 2 * j + i],
                )
                copy.start()
                loads.append(copy)
        bias = bias_ref[0, :, pl.ds(block * size, size)]
        high = bias.astype(BF16).astype(F32)
        middle = (bias - high).astype(BF16).astype(F32)
        low = bias - high - middle
        packed = jnp.concatenate([high, middle, low, jnp.zeros((10, size), F32)], axis=0)
        pieces[d][4 * size : 4 * size + 16] = packed.astype(BF16)

    half = Z * table.shape[1]
    line = lax.broadcasted_iota(jnp.int32, (half, size), 0)
    zero_mode = jnp.logical_and(jnp.logical_and(line < 8, (line & 1) == 0), core == 0)
    factor = jnp.where(zero_mode, 1.0, 2.0).astype(F32)
    for copy in copies:
        copy.wait()
    high = table[:, :, :depth].reshape(half, depth)
    low = table[:, :, depth:].reshape(half, depth)
    for k in range(2):
        part = field[:, k * size : (k + 1) * size]
        spectrum = ((dot(high, part) + dot(low, part)) * factor).astype(BF16).reshape(Z, 2, 8, size)
        for m in range(2):
            out_ref[:, 2 * m + k] = spectrum[:, m]
    for copy in loads:
        copy.wait()


def row_kernel(table_ref, act_ref, rows_ref):
    size = rows_ref.shape[6]
    for n in range(2 * Y):
        spectrum = twice(table_ref, act_ref[:, n * size : (n + 1) * size]).astype(BF16)
        rows_ref[:, :, :, n % 2, n // 2] = spectrum.reshape(Z, 2, 2, 8, size)


def turn_kernel(arrived_ref, *outs):
    x = lax.axis_index("x")
    for e in range(X):
        outs[e][...] = arrived_ref[:, (x + e) & (X - 1)]


def inverse_kernel(table_ref, spec_ref, cot_ref, out_ref, result, sems):
    rows = table_ref.shape[0]
    size = spec_ref.shape[6]
    copies = []
    for n in range(2 * Y):
        block = slice(n * size, (n + 1) * size)
        field = twice(table_ref, spec_ref[:, :, :, n % 2, n // 2].reshape(rows, size))
        result[:, block] = (field + cot_ref[:, block].astype(F32)).astype(BF16)
        copy = pltpu.make_async_copy(result.at[:, block], out_ref.at[:, block], sems.at[n])
        copy.start()
        copies.append(copy)
    for copy in copies:
        copy.wait()


def chain_kernel(act_ref, col_ref, inv_ref, fold_ref, *rest):
    sections = 2 * Y
    cots, weights = rest[:X], rest[X : X + sections]
    out_ref, found, held, sems = rest[X + sections :]
    size = act_ref.shape[6]
    half = col_ref.shape[0] // 2
    y, core, x, z = (lax.axis_index(name) for name in ("y", "core", "x", "z"))

    def load(p, source):
        return pltpu.make_async_copy(weights[source], held.at[p], sems.at[p])

    for here in range(sections):

        @pl.when(y * 2 + core == here)
        def _():
            for p in range(sections - 1, -1, -1):
                load(p, 2 * ((here // 2 - p // 2) % Y) + (p % 2 != here % 2)).start()

    for e in range(X):
        found[:, (x - e) & (X - 1)] = cots[e][...]
    has_zero = jnp.logical_and(jnp.logical_and(core == 0, x < 2), z == 0)
    fold = jnp.where(has_zero, 1, 0)

    base = twice(col_ref, found[...].reshape(2 * half, size))
    total = jnp.zeros_like(base)
    height_total = jnp.zeros_like(base)
    grad = base.astype(BF16)
    spectra = []
    for p in range(sections):
        columns = act_ref[:, p % 2, :, :, p // 2].reshape(2 * half, size)
        spectra.append(twice(col_ref, columns).astype(BF16))

    for p in range(sections - 1, -1, -1):
        load(p, 0).wait()
        a_re, a_im = held[p, 0:size], held[p, size : 2 * size]
        b_re, b_im = held[p, 2 * size : 3 * size], held[p, 3 * size : 4 * size]
        bias = held[p, 4 * size : 4 * size + 16].astype(F32)
        bias_re = bias[0:1] + bias[2:3] + bias[4:5]
        bias_im = bias[1:2] + bias[3:4] + bias[5:6]
        s = spectra[p]
        s_turned = jnp.concatenate([-s[half:], s[:half]], axis=0)
        z_both = dot(s, a_re) + dot(s_turned, a_im)
        slope = gelu_slope(jnp.concatenate([z_both[:half] + bias_re, z_both[half:] + bias_im], axis=0))
        g_turned = jnp.concatenate([grad[half:], -grad[:half]], axis=0)
        u = dot_t(grad, b_re) + dot_t(g_turned, b_im)
        q = (u * slope).astype(BF16)
        q_turned = jnp.concatenate([q[half:], -q[:half]], axis=0)
        e = (dot_t(q, a_re) + dot_t(q_turned, a_im)).astype(BF16)
        height_total = height_total + twice(inv_ref, e)
        out_ref[:, p % 2, :, :, p // 2] = height_total.astype(BF16).reshape(Z, 2, 2, 8, size)
        if p > 0:
            total = total + dot(fold_ref[fold], e)
            grad = (base + total).astype(BF16)


def body(activations, cotangent, w_first, w_second, b_first):
    sections, columns = 2 * Y, X * Z
    _, rows, width, channels = activations.shape
    size = w_first.shape[3]
    height = rows * columns
    pair = width // 2 // columns
    count = rows * width
    tile = 2 * rows * pair
    row_table = row_matrix(rows, width, columns)
    row_table = row_table.reshape(2, 2, Z, -1).transpose(2, 0, 1, 3).reshape(row_table.shape)
    forward_rows, inverse_rows = two_parts(row_table), two_parts(row_table.T)
    column_table = column_matrix(height, pair)
    column_table = column_table.reshape(-1, X, Z, tile).transpose(0, 2, 1, 3).reshape(column_table.shape)
    forward_columns, inverse_columns = two_parts(column_table), two_parts(column_table.T)
    folds = fold_matrices(height, pair)

    vmem = pl.BlockSpec(memory_space=pltpu.VMEM)
    hbm = pl.BlockSpec(memory_space=pl.ANY)
    blocks = (Z, 2, 2, 2, Y, tile, size)

    def shaped(*dims):
        return pltpu.VMEM(dims, BF16)

    def near(*values):
        return [pltpu.with_memory_space_constraint(value, pltpu.VMEM) for value in values]

    def far(*values):
        return [pltpu.with_memory_space_constraint(value, pltpu.HBM) for value in values]

    def exchange(value):
        flat = value.reshape(sections * columns, tile, size)
        return lax.all_to_all(flat, EVERYONE, split_axis=0, concat_axis=0, tiled=True).reshape(blocks)

    def shifted(value, axis, distance):
        size = lax.axis_size(axis)
        return lax.ppermute(value, axis, [(i, (i + distance) % size) for i in range(size)])

    flat_cot = cotangent.reshape(count, channels)
    made = pl.pallas_call(
        first_kernel,
        in_specs=[hbm] * 4 + [vmem],
        out_specs=[vmem] * (Y + 1),
        out_shape=[shaped(4 * size + 16, size)] * Y + [shaped(Z, X, tile, size)],
        scratch_shapes=[
            pltpu.VMEM((Z, 2 * tile, 2 * count), BF16),
            pltpu.VMEM((count, 2 * size), BF16),
            pltpu.SemaphoreType.DMA((Y, 4)),
            pltpu.SemaphoreType.DMA((2,)),
        ],
        compiler_params=SMALL,
        name="first",
    )(*far(jnp.asarray(forward_rows.reshape(Z, 2, 2 * tile, -1)), flat_cot, w_first, w_second), b_first)
    pieces, cot_rows = made[:Y], made[Y]
    cot_blocks = lax.all_to_all(
        cot_rows.reshape(Z, X * tile, size), "z", split_axis=0, concat_axis=0, tiled=True
    ).reshape(cot_rows.shape)
    act_rows = pl.pallas_call(
        row_kernel,
        in_specs=[vmem] * 2,
        out_specs=vmem,
        out_shape=shaped(*blocks),
        compiler_params=SMALL,
        name="act_rows",
    )(*near(jnp.asarray(forward_rows), activations.reshape(count, channels)))

    weights = []
    for d in range(Y):
        piece = shifted(pieces[d], "y", d) if d else pieces[0]
        weights += [piece, shifted(piece, "core", 1)]
    act_columns = exchange(act_rows)
    turned = pl.pallas_call(
        turn_kernel,
        in_specs=[vmem],
        out_specs=[vmem] * X,
        out_shape=[shaped(Z, tile, size)] * X,
        compiler_params=SMALL,
        name="turn",
    )(*near(cot_blocks))
    cots = [turned[0]] + [shifted(turned[e], "x", e) for e in range(1, X)]

    tables = [jnp.asarray(table) for table in (forward_columns, inverse_columns, folds)]
    back = pl.pallas_call(
        chain_kernel,
        in_specs=[vmem] * (4 + X) + [hbm] * sections,
        out_specs=vmem,
        out_shape=shaped(*blocks),
        scratch_shapes=[
            pltpu.VMEM((Z, X, tile, size), BF16),
            pltpu.VMEM((sections, 4 * size + 16, size), BF16),
            pltpu.SemaphoreType.DMA((sections,)),
        ],
        compiler_params=SMALL,
        name="chain",
    )(*near(act_columns, *tables, *cots), *far(*weights))
    grads = pl.pallas_call(
        inverse_kernel,
        in_specs=[vmem] * 3,
        out_specs=hbm,
        out_shape=jax.ShapeDtypeStruct((count, channels), BF16),
        scratch_shapes=[pltpu.VMEM((count, channels), BF16), pltpu.SemaphoreType.DMA((sections,))],
        compiler_params=SMALL,
        name="inverse_rows",
    )(*near(jnp.asarray(inverse_rows), exchange(back), flat_cot))
    return grads.reshape(1, rows, width, channels)


def solution(mesh):
    chips = Mesh(mesh.devices.reshape(Y, 2, X, Z), ("y", "core", "x", "z"))
    pipe, space = ("y", "core"), ("x", "z")
    in_specs = (
        P(pipe, space, None, None),
        P(space, None, None),
        P(pipe, None, None, None, None),
        P(pipe, None, None, None, None),
        P(pipe, None, None),
    )
    out_specs = P(pipe, space, None, None)
    return jax.shard_map(body, mesh=chips, in_specs=in_specs, out_specs=out_specs, check_vma=False)
```

```python
import math

import jax
import jax.numpy as jnp
import numpy as np
from jax import lax
from jax.experimental import pallas as pl
from jax.experimental.pallas import tpu as pltpu
from jax.sharding import Mesh
from jax.sharding import PartitionSpec as P


BF16 = jnp.bfloat16
F32 = jnp.float32
X, Y, Z = 4, 4, 8
SMALL = pltpu.CompilerParams(vmem_limit_bytes=20 << 20)
TIGHT = pltpu.CompilerParams(vmem_limit_bytes=20 << 20)
EVERYONE = ("z", "core", "x", "y")


def two_parts(table):
    high = table.astype(np.float32).astype(BF16)
    low = (table - high.astype(np.float64)).astype(np.float32).astype(BF16)
    return np.concatenate([high, low], axis=1)


def row_matrix(rows, width, columns):
    modes = width // 2
    pair = modes // columns
    angles = 2.0 * math.pi * (np.outer(np.arange(modes), np.arange(width)) % width) / width
    scale = 1.0 / math.sqrt(width)
    parts = np.stack([np.cos(angles), -np.sin(angles)]) * scale
    table = np.zeros((columns, rows, 2, pair, rows, width))
    by_column = parts.reshape(2, columns, pair, width).transpose(1, 0, 2, 3)
    for h in range(rows):
        table[:, h, :, :, h, :] = by_column
    return table.reshape(columns * rows * 2 * pair, rows * width)


def column_matrix(height, pair):
    angles = 2.0 * math.pi * (np.outer(np.arange(height), np.arange(height)) % height) / height
    scale = 1.0 / math.sqrt(height)
    cosines, sines = np.cos(angles) * scale, np.sin(angles) * scale
    table = np.zeros((2, pair, height, height, 2, pair))
    for k in range(pair):
        table[0, k, :, :, 0, k] = cosines
        table[0, k, :, :, 1, k] = sines
        table[1, k, :, :, 1, k] = cosines
        table[1, k, :, :, 0, k] = -sines
    return table.reshape(2 * pair * height, 2 * pair * height)


def fold_matrices(height, pair):
    size = 2 * pair * height
    plain = np.eye(size)
    folded = np.eye(size).reshape(2, pair, height, 2, pair, height)
    eye = np.eye(height)
    flip = eye[(-np.arange(height)) % height]
    folded[0, 0, :, 0, 0, :] = 0.5 * (eye + flip)
    folded[1, 0, :, 1, 0, :] = 0.5 * (eye - flip)
    return np.stack([plain, folded.reshape(size, size)]).astype(np.float32).astype(BF16)


def dot(left, right):
    return jnp.dot(left, right, preferred_element_type=F32)


def dot_t(left, right):
    return lax.dot_general(left, right, (((1,), (1,)), ((), ())), preferred_element_type=F32)


def gelu_slope(values):
    return (
        0.5 * (1.0 + lax.erf(values * 0.7071067811865476))
        + values * jnp.exp(-0.5 * values * values) * 0.3989422804014327
    )


def twice(table_ref, operand):
    depth = operand.shape[0]
    return dot(table_ref[:, :depth], operand) + dot(table_ref[:, depth:], operand)


def cot_kernel(table_ref, cot_ref, out_ref, table, field, sems):
    size = out_ref.shape[3]
    depth = table.shape[2] // 2
    y, core = lax.axis_index("y"), lax.axis_index("core")
    copies = [
        pltpu.make_async_copy(table_ref.at[:, core], table, sems.at[0]),
        pltpu.make_async_copy(cot_ref.at[:, pl.ds(y * 2 * size, 2 * size)], field, sems.at[1]),
    ]
    for copy in copies:
        copy.start()
    half = Z * table.shape[1]
    line = lax.broadcasted_iota(jnp.int32, (half, size), 0)
    zero_mode = jnp.logical_and(jnp.logical_and(line < 8, (line & 1) == 0), core == 0)
    factor = jnp.where(zero_mode, 1.0, 2.0).astype(F32)
    for copy in copies:
        copy.wait()
    high = table[:, :, :depth].reshape(half, depth)
    low = table[:, :, depth:].reshape(half, depth)
    for k in range(2):
        part = field[:, k * size : (k + 1) * size]
        spectrum = ((dot(high, part) + dot(low, part)) * factor).astype(BF16).reshape(Z, 2, 8, size)
        for m in range(2):
            out_ref[:, 2 * m + k] = spectrum[:, m]


def prologue_kernel(table_ref, act_ref, first_ref, second_ref, bias_ref, *rest):
    pieces = rest[:Y]
    rows_ref, held, biases, sems, bias_sem = rest[Y:]
    size = held.shape[2]
    y, odd = lax.axis_index("y"), lax.axis_index("x") & 1
    bias_copy = pltpu.make_async_copy(bias_ref, biases, bias_sem)
    bias_copy.start()
    loads = []
    for d in range(Y):
        block = ((y + d) & (Y - 1)) * 2 + odd
        for i in range(2):
            for j, ref in enumerate((first_ref, second_ref)):
                copy = pltpu.make_async_copy(
                    ref.at[0, i, block],
                    held.at[d, pl.ds((2 * j + i) * size, size)],
                    sems.at[d, 2 * j + i],
                )
                copy.start()
                loads.append(copy)

    def transform(n):
        spectrum = twice(table_ref, act_ref[:, n * size : (n + 1) * size]).astype(BF16)
        rows_ref[:, :, :, n % 2, n // 2] = spectrum.reshape(Z, 2, 2, 8, size)

    for n in range(4):
        transform(n)
    bias_copy.wait()
    for d in range(Y):
        block = ((y + d) & (Y - 1)) * 2 + odd
        bias = biases[0, :, pl.ds(block * size, size)]
        high = bias.astype(BF16).astype(F32)
        middle = (bias - high).astype(BF16).astype(F32)
        low = bias - high - middle
        packed = jnp.concatenate([high, middle, low, jnp.zeros((10, size), F32)], axis=0)
        held[d, 4 * size : 4 * size + 16] = packed.astype(BF16)
    for copy in loads:
        copy.wait()
    stores = []
    for d in range(Y):
        copy = pltpu.make_async_copy(held.at[d], pieces[d], sems.at[d, 4])
        copy.start()
        stores.append(copy)
    for n in range(4, 2 * Y):
        transform(n)
    for copy in stores:
        copy.wait()


def turn_kernel(arrived_ref, *outs):
    x = lax.axis_index("x")
    for e in range(X):
        outs[e][...] = arrived_ref[:, (x + e) & (X - 1)]


def inverse_kernel(table_ref, spec_ref, cot_ref, out_ref, result, sems):
    rows = table_ref.shape[0]
    size = spec_ref.shape[6]
    copies = []
    for n in range(2 * Y):
        block = slice(n * size, (n + 1) * size)
        field = twice(table_ref, spec_ref[:, :, :, n % 2, n // 2].reshape(rows, size))
        result[:, block] = (field + cot_ref[:, block].astype(F32)).astype(BF16)
        copy = pltpu.make_async_copy(result.at[:, block], out_ref.at[:, block], sems.at[n])
        copy.start()
        copies.append(copy)
    for copy in copies:
        copy.wait()


def chain_kernel(act_ref, col_ref, inv_ref, fold_ref, *rest):
    sections = 2 * Y
    cots, weights = rest[:X], rest[X : X + sections]
    out_ref, found, held, sems = rest[X + sections :]
    size = act_ref.shape[6]
    half = col_ref.shape[0] // 2
    y, core, x, z = (lax.axis_index(name) for name in ("y", "core", "x", "z"))

    def load(p, source):
        return pltpu.make_async_copy(weights[source], held.at[p], sems.at[p])

    for here in range(sections):

        @pl.when(y * 2 + core == here)
        def _():
            for p in range(sections - 1, -1, -1):
                load(p, 2 * ((here // 2 - p // 2) % Y) + (p % 2 != here % 2)).start()

    for e in range(X):
        found[:, (x - e) & (X - 1)] = cots[e][...]
    has_zero = jnp.logical_and(jnp.logical_and(core == 0, x < 2), z == 0)
    fold = jnp.where(has_zero, 1, 0)

    base = twice(col_ref, found[...].reshape(2 * half, size))
    total = jnp.zeros_like(base)
    height_total = jnp.zeros_like(base)
    grad = base.astype(BF16)
    spectra = []
    for p in range(sections):
        columns = act_ref[:, p % 2, :, :, p // 2].reshape(2 * half, size)
        spectra.append(twice(col_ref, columns).astype(BF16))

    for p in range(sections - 1, -1, -1):
        load(p, 0).wait()
        a_re, a_im = held[p, 0:size], held[p, size : 2 * size]
        b_re, b_im = held[p, 2 * size : 3 * size], held[p, 3 * size : 4 * size]
        bias = held[p, 4 * size : 4 * size + 16].astype(F32)
        bias_re = bias[0:1] + bias[2:3] + bias[4:5]
        bias_im = bias[1:2] + bias[3:4] + bias[5:6]
        s = spectra[p]
        s_turned = jnp.concatenate([-s[half:], s[:half]], axis=0)
        z_both = dot(s, a_re) + dot(s_turned, a_im)
        slope = gelu_slope(jnp.concatenate([z_both[:half] + bias_re, z_both[half:] + bias_im], axis=0))
        g_turned = jnp.concatenate([grad[half:], -grad[:half]], axis=0)
        u = dot_t(grad, b_re) + dot_t(g_turned, b_im)
        q = (u * slope).astype(BF16)
        q_turned = jnp.concatenate([q[half:], -q[:half]], axis=0)
        e = (dot_t(q, a_re) + dot_t(q_turned, a_im)).astype(BF16)
        height_total = height_total + twice(inv_ref, e)
        out_ref[:, p % 2, :, :, p // 2] = height_total.astype(BF16).reshape(Z, 2, 2, 8, size)
        if p > 0:
            total = total + dot(fold_ref[fold], e)
            grad = (base + total).astype(BF16)


def body(activations, cotangent, w_first, w_second, b_first):
    sections, columns = 2 * Y, X * Z
    _, rows, width, channels = activations.shape
    size = w_first.shape[3]
    height = rows * columns
    pair = width // 2 // columns
    count = rows * width
    tile = 2 * rows * pair
    row_table = row_matrix(rows, width, columns)
    row_table = row_table.reshape(2, 2, Z, -1).transpose(2, 0, 1, 3).reshape(row_table.shape)
    forward_rows, inverse_rows = two_parts(row_table), two_parts(row_table.T)
    column_table = column_matrix(height, pair)
    column_table = column_table.reshape(-1, X, Z, tile).transpose(0, 2, 1, 3).reshape(column_table.shape)
    forward_columns, inverse_columns = two_parts(column_table), two_parts(column_table.T)
    folds = fold_matrices(height, pair)

    vmem = pl.BlockSpec(memory_space=pltpu.VMEM)
    hbm = pl.BlockSpec(memory_space=pl.ANY)
    blocks = (Z, 2, 2, 2, Y, tile, size)

    def shaped(*dims):
        return pltpu.VMEM(dims, BF16)

    def near(*values):
        return [pltpu.with_memory_space_constraint(value, pltpu.VMEM) for value in values]

    def far(*values):
        return [pltpu.with_memory_space_constraint(value, pltpu.HBM) for value in values]

    def exchange(value):
        flat = value.reshape(sections * columns, tile, size)
        return lax.all_to_all(flat, EVERYONE, split_axis=0, concat_axis=0, tiled=True).reshape(blocks)

    def shifted(value, axis, distance):
        size = lax.axis_size(axis)
        return lax.ppermute(value, axis, [(i, (i + distance) % size) for i in range(size)])

    flat_cot = cotangent.reshape(count, channels)
    cot_rows = pl.pallas_call(
        cot_kernel,
        in_specs=[hbm] * 2,
        out_specs=vmem,
        out_shape=shaped(Z, X, tile, size),
        scratch_shapes=[
            pltpu.VMEM((Z, 2 * tile, 2 * count), BF16),
            pltpu.VMEM((count, 2 * size), BF16),
            pltpu.SemaphoreType.DMA((2,)),
        ],
        compiler_params=SMALL,
        name="cot_rows",
    )(*far(jnp.asarray(forward_rows.reshape(Z, 2, 2 * tile, -1)), flat_cot))
    cot_blocks = lax.all_to_all(
        cot_rows.reshape(Z, X * tile, size), "z", split_axis=0, concat_axis=0, tiled=True
    ).reshape(cot_rows.shape)
    made = pl.pallas_call(
        prologue_kernel,
        in_specs=[vmem] * 2 + [hbm] * 3,
        out_specs=[hbm] * Y + [vmem],
        out_shape=[pltpu.HBM((4 * size + 16, size), BF16)] * Y + [shaped(*blocks)],
        scratch_shapes=[
            pltpu.VMEM((Y, 4 * size + 16, size), BF16),
            pltpu.VMEM(b_first.shape, F32),
            pltpu.SemaphoreType.DMA((Y, 5)),
            pltpu.SemaphoreType.DMA(()),
        ],
        compiler_params=SMALL,
        name="prologue",
    )(
        *near(jnp.asarray(forward_rows), activations.reshape(count, channels)),
        *far(w_first, w_second, b_first),
    )
    pieces, act_rows = made[:Y], made[Y]

    weights = []
    for d in range(Y):
        piece = shifted(pieces[d], "y", d) if d else pieces[0]
        weights += [piece, shifted(piece, "core", 1)]
    act_columns = exchange(act_rows)
    turned = pl.pallas_call(
        turn_kernel,
        in_specs=[vmem],
        out_specs=[vmem] * X,
        out_shape=[shaped(Z, tile, size)] * X,
        compiler_params=SMALL,
        name="turn",
    )(*near(cot_blocks))
    cots = [turned[0]] + [shifted(turned[e], "x", e) for e in range(1, X)]

    tables = [jnp.asarray(table) for table in (forward_columns, inverse_columns, folds)]
    back = pl.pallas_call(
        chain_kernel,
        in_specs=[vmem] * (4 + X) + [hbm] * sections,
        out_specs=vmem,
        out_shape=shaped(*blocks),
        scratch_shapes=[
            pltpu.VMEM((Z, X, tile, size), BF16),
            pltpu.VMEM((sections, 4 * size + 16, size), BF16),
            pltpu.SemaphoreType.DMA((sections,)),
        ],
        compiler_params=TIGHT,
        name="chain",
    )(*near(act_columns, *tables, *cots), *far(*weights))
    grads = pl.pallas_call(
        inverse_kernel,
        in_specs=[vmem] * 3,
        out_specs=hbm,
        out_shape=jax.ShapeDtypeStruct((count, channels), BF16),
        scratch_shapes=[pltpu.VMEM((count, channels), BF16), pltpu.SemaphoreType.DMA((sections,))],
        compiler_params=SMALL,
        name="inverse_rows",
    )(*near(jnp.asarray(inverse_rows), exchange(back), flat_cot))
    return grads.reshape(1, rows, width, channels)


def solution(mesh):
    chips = Mesh(mesh.devices.reshape(Y, 2, X, Z), ("y", "core", "x", "z"))
    pipe, space = ("y", "core"), ("x", "z")
    in_specs = (
        P(pipe, space, None, None),
        P(space, None, None),
        P(pipe, None, None, None, None),
        P(pipe, None, None, None, None),
        P(pipe, None, None),
    )
    out_specs = P(pipe, space, None, None)
    return jax.shard_map(body, mesh=chips, in_specs=in_specs, out_specs=out_specs, check_vma=False)
```

```python
import math

import jax
import jax.numpy as jnp
import numpy as np
from jax import lax
from jax.experimental import pallas as pl
from jax.experimental.pallas import tpu as pltpu
from jax.sharding import Mesh
from jax.sharding import PartitionSpec as P


BF16 = jnp.bfloat16
F32 = jnp.float32
X, Y, Z = 4, 4, 8
SMALL = pltpu.CompilerParams(vmem_limit_bytes=20 << 20)
TIGHT = pltpu.CompilerParams(vmem_limit_bytes=20 << 20)
EVERYONE = ("z", "core", "x", "y")


def two_parts(table):
    high = table.astype(np.float32).astype(BF16)
    low = (table - high.astype(np.float64)).astype(np.float32).astype(BF16)
    return np.concatenate([high, low], axis=1)


def row_matrix(rows, width, columns):
    modes = width // 2
    pair = modes // columns
    angles = 2.0 * math.pi * (np.outer(np.arange(modes), np.arange(width)) % width) / width
    scale = 1.0 / math.sqrt(width)
    parts = np.stack([np.cos(angles), -np.sin(angles)]) * scale
    table = np.zeros((columns, rows, 2, pair, rows, width))
    by_column = parts.reshape(2, columns, pair, width).transpose(1, 0, 2, 3)
    for h in range(rows):
        table[:, h, :, :, h, :] = by_column
    return table.reshape(columns * rows * 2 * pair, rows * width)


def column_matrix(height, pair):
    angles = 2.0 * math.pi * (np.outer(np.arange(height), np.arange(height)) % height) / height
    scale = 1.0 / math.sqrt(height)
    cosines, sines = np.cos(angles) * scale, np.sin(angles) * scale
    table = np.zeros((2, pair, height, height, 2, pair))
    for k in range(pair):
        table[0, k, :, :, 0, k] = cosines
        table[0, k, :, :, 1, k] = sines
        table[1, k, :, :, 1, k] = cosines
        table[1, k, :, :, 0, k] = -sines
    return table.reshape(2 * pair * height, 2 * pair * height)


def fold_matrices(height, pair):
    size = 2 * pair * height
    plain = np.eye(size)
    folded = np.eye(size).reshape(2, pair, height, 2, pair, height)
    eye = np.eye(height)
    flip = eye[(-np.arange(height)) % height]
    folded[0, 0, :, 0, 0, :] = 0.5 * (eye + flip)
    folded[1, 0, :, 1, 0, :] = 0.5 * (eye - flip)
    return np.stack([plain, folded.reshape(size, size)]).astype(np.float32).astype(BF16)


def dot(left, right):
    return jnp.dot(left, right, preferred_element_type=F32)


def dot_t(left, right):
    return lax.dot_general(left, right, (((1,), (1,)), ((), ())), preferred_element_type=F32)


def gelu_slope(values):
    return (
        0.5 * (1.0 + lax.erf(values * 0.7071067811865476))
        + values * jnp.exp(-0.5 * values * values) * 0.3989422804014327
    )


def twice(table_ref, operand):
    depth = operand.shape[0]
    return dot(table_ref[:, :depth], operand) + dot(table_ref[:, depth:], operand)


def cot_kernel(table_ref, cot_ref, *rest):
    outs, table, field, sems = rest[:2], rest[2], rest[3], rest[4]
    size = outs[0].shape[3]
    depth = table.shape[2] // 2
    y, core, z = (lax.axis_index(name) for name in ("y", "core", "z"))
    targets = [(z + y + 4 * i) & (Z - 1) for i in range(2)]
    copies = [
        pltpu.make_async_copy(table_ref.at[targets[0], core], table.at[0], sems.at[0]),
        pltpu.make_async_copy(table_ref.at[targets[1], core], table.at[1], sems.at[1]),
        pltpu.make_async_copy(cot_ref, field, sems.at[2]),
    ]
    for copy in copies:
        copy.start()
    lines = table.shape[1]
    line = lax.broadcasted_iota(jnp.int32, (lines, size), 0)
    first_even = jnp.logical_and(line < 8, (line & 1) == 0)
    factors = []
    for target in targets:
        zero_mode = jnp.logical_and(first_even, jnp.logical_and(target == 0, core == 0))
        factors.append(jnp.where(zero_mode, 1.0, 2.0).astype(F32))
    for copy in copies:
        copy.wait()
    rows = jnp.concatenate([table[0, :, :depth], table[1, :, :depth], table[0, :, depth:], table[1, :, depth:]], axis=0)
    for n in range(2 * Y):
        spectrum = dot(rows, field[:, n * size : (n + 1) * size])
        spectrum = spectrum[: 2 * lines] + spectrum[2 * lines :]
        for i in range(2):
            tiles = (spectrum[i * lines : (i + 1) * lines] * factors[i]).astype(BF16)
            for m in range(2):
                outs[i][n // 2, 2 * m + n % 2] = tiles[m * 8 : (m + 1) * 8]


def prologue_kernel(table_hbm, act_hbm, first_ref, second_ref, bias_ref, *rest):
    pieces = rest[:Y]
    rows_ref, table_ref, act_ref, held, biases, sems, own_sems = rest[Y:]
    size = held.shape[2]
    y, odd = lax.axis_index("y"), lax.axis_index("x") & 1
    sources = (table_hbm, act_hbm, bias_ref)
    own = [
        pltpu.make_async_copy(source, target, own_sems.at[k])
        for k, (source, target) in enumerate(zip(sources, (table_ref, act_ref, biases)))
    ]
    for copy in own:
        copy.start()
    loads = []
    for d in range(Y):
        block = ((y + d) & (Y - 1)) * 2 + odd
        for i in range(2):
            for j, ref in enumerate((first_ref, second_ref)):
                copy = pltpu.make_async_copy(
                    ref.at[0, i, block],
                    held.at[d, pl.ds((2 * j + i) * size, size)],
                    sems.at[d, 2 * j + i],
                )
                copy.start()
                loads.append(copy)

    def transform(n):
        spectrum = twice(table_ref, act_ref[:, n * size : (n + 1) * size]).astype(BF16)
        rows_ref[:, :, :, n % 2, n // 2] = spectrum.reshape(Z, 2, 2, 8, size)

    for copy in own:
        copy.wait()
    for n in range(4):
        transform(n)
    for d in range(Y):
        block = ((y + d) & (Y - 1)) * 2 + odd
        bias = biases[0, :, pl.ds(block * size, size)]
        high = bias.astype(BF16).astype(F32)
        middle = (bias - high).astype(BF16).astype(F32)
        low = bias - high - middle
        packed = jnp.concatenate([high, middle, low, jnp.zeros((10, size), F32)], axis=0)
        held[d, 4 * size : 4 * size + 16] = packed.astype(BF16)
    for copy in loads:
        copy.wait()
    stores = []
    for d in range(Y):
        copy = pltpu.make_async_copy(held.at[d], pieces[d], sems.at[d, 4])
        copy.start()
        stores.append(copy)
    for n in range(4, 2 * Y):
        transform(n)
    for copy in stores:
        copy.wait()


def turn_y_kernel(*refs):
    arrived, outs = refs[:2], refs[2:]
    y = lax.axis_index("y")
    for d in range(Y):
        for i in range(2):
            outs[d][i] = arrived[i][(y + d) & (Y - 1)]


def turn_x_kernel(*refs):
    arrived, outs = refs[:Y], refs[Y:]
    x = lax.axis_index("x")
    for e in range(X):
        for d in range(Y):
            outs[e][d] = arrived[d][:, (x + e) & (X - 1)]


def inverse_kernel(table_ref, spec_ref, cot_ref, out_ref, result, sems):
    rows = table_ref.shape[0]
    size = spec_ref.shape[6]
    copies = []
    for n in range(2 * Y):
        block = slice(n * size, (n + 1) * size)
        field = twice(table_ref, spec_ref[:, :, :, n % 2, n // 2].reshape(rows, size))
        result[:, block] = (field + cot_ref[:, block].astype(F32)).astype(BF16)
        copy = pltpu.make_async_copy(result.at[:, block], out_ref.at[:, block], sems.at[n])
        copy.start()
        copies.append(copy)
    for copy in copies:
        copy.wait()


def chain_kernel(act_ref, col_ref, inv_ref, fold_ref, *rest):
    sections = 2 * Y
    cots, weights = rest[:X], rest[X : X + sections]
    out_ref, found, held, sems = rest[X + sections :]
    size = act_ref.shape[6]
    half = col_ref.shape[0] // 2
    y, core, x, z = (lax.axis_index(name) for name in ("y", "core", "x", "z"))

    def load(p, source):
        return pltpu.make_async_copy(weights[source], held.at[p], sems.at[p])

    for here in range(sections):

        @pl.when(y * 2 + core == here)
        def _():
            for p in range(sections - 1, -1, -1):
                load(p, 2 * ((here // 2 - p // 2) % Y) + (p % 2 != here % 2)).start()

    for e in range(X):
        for d in range(Y):
            for i in range(2):
                found[(z - ((y - d) & (Y - 1)) - 4 * i) & (Z - 1), (x - e) & (X - 1)] = cots[e][d, i]
    has_zero = jnp.logical_and(jnp.logical_and(core == 0, x < 2), z == 0)
    fold = jnp.where(has_zero, 1, 0)

    base = twice(col_ref, found[...].reshape(2 * half, size))
    total = jnp.zeros_like(base)
    height_total = jnp.zeros_like(base)
    grad = base.astype(BF16)
    spectra = []
    for p in range(sections):
        columns = act_ref[:, p % 2, :, :, p // 2].reshape(2 * half, size)
        spectra.append(twice(col_ref, columns).astype(BF16))

    for p in range(sections - 1, -1, -1):
        load(p, 0).wait()
        a_re, a_im = held[p, 0:size], held[p, size : 2 * size]
        b_re, b_im = held[p, 2 * size : 3 * size], held[p, 3 * size : 4 * size]
        bias = held[p, 4 * size : 4 * size + 16].astype(F32)
        bias_re = bias[0:1] + bias[2:3] + bias[4:5]
        bias_im = bias[1:2] + bias[3:4] + bias[5:6]
        s = spectra[p]
        s_turned = jnp.concatenate([-s[half:], s[:half]], axis=0)
        z_both = dot(s, a_re) + dot(s_turned, a_im)
        slope = gelu_slope(jnp.concatenate([z_both[:half] + bias_re, z_both[half:] + bias_im], axis=0))
        g_turned = jnp.concatenate([grad[half:], -grad[:half]], axis=0)
        u = dot_t(grad, b_re) + dot_t(g_turned, b_im)
        q = (u * slope).astype(BF16)
        q_turned = jnp.concatenate([q[half:], -q[:half]], axis=0)
        e = (dot_t(q, a_re) + dot_t(q_turned, a_im)).astype(BF16)
        height_total = height_total + twice(inv_ref, e)
        out_ref[:, p % 2, :, :, p // 2] = height_total.astype(BF16).reshape(Z, 2, 2, 8, size)
        if p > 0:
            total = total + dot(fold_ref[fold], e)
            grad = (base + total).astype(BF16)


def body(activations, cotangent, w_first, w_second, b_first):
    sections, columns = 2 * Y, X * Z
    _, rows, width, channels = activations.shape
    size = w_first.shape[3]
    height = rows * columns
    pair = width // 2 // columns
    count = rows * width
    tile = 2 * rows * pair
    row_table = row_matrix(rows, width, columns)
    row_table = row_table.reshape(2, 2, Z, -1).transpose(2, 0, 1, 3).reshape(row_table.shape)
    forward_rows, inverse_rows = two_parts(row_table), two_parts(row_table.T)
    column_table = column_matrix(height, pair)
    column_table = column_table.reshape(-1, X, Z, tile).transpose(0, 2, 1, 3).reshape(column_table.shape)
    forward_columns, inverse_columns = two_parts(column_table), two_parts(column_table.T)
    folds = fold_matrices(height, pair)

    vmem = pl.BlockSpec(memory_space=pltpu.VMEM)
    hbm = pl.BlockSpec(memory_space=pl.ANY)
    blocks = (Z, 2, 2, 2, Y, tile, size)

    def shaped(*dims):
        return pltpu.VMEM(dims, BF16)

    def near(*values):
        return [pltpu.with_memory_space_constraint(value, pltpu.VMEM) for value in values]

    def far(*values):
        return [pltpu.with_memory_space_constraint(value, pltpu.HBM) for value in values]

    def exchange(value):
        flat = value.reshape(sections * columns, tile, size)
        return lax.all_to_all(flat, EVERYONE, split_axis=0, concat_axis=0, tiled=True).reshape(blocks)

    def shifted(value, axis, distance):
        size = lax.axis_size(axis)
        return lax.ppermute(value, axis, [(i, (i + distance) % size) for i in range(size)])

    flat_cot = cotangent.reshape(count, channels)
    cot_rows = pl.pallas_call(
        cot_kernel,
        in_specs=[hbm] * 2,
        out_specs=[vmem] * 2,
        out_shape=[shaped(Y, X, tile, size)] * 2,
        scratch_shapes=[
            pltpu.VMEM((2, 2 * tile, 2 * count), BF16),
            pltpu.VMEM((count, channels), BF16),
            pltpu.SemaphoreType.DMA((3,)),
        ],
        compiler_params=SMALL,
        name="cot_rows",
    )(*far(jnp.asarray(forward_rows.reshape(Z, 2, 2 * tile, -1)), flat_cot))
    arrived = []
    for i in range(2):
        route = [(y * Z + z, y * Z + (z + y + 4 * i) % Z) for y in range(Y) for z in range(Z)]
        arrived.append(lax.ppermute(cot_rows[i], ("y", "z"), route))
    made = pl.pallas_call(
        prologue_kernel,
        in_specs=[hbm] * 5,
        out_specs=[hbm] * Y + [vmem],
        out_shape=[pltpu.HBM((4 * size + 16, size), BF16)] * Y + [shaped(*blocks)],
        scratch_shapes=[
            pltpu.VMEM(forward_rows.shape, BF16),
            pltpu.VMEM((count, channels), BF16),
            pltpu.VMEM((Y, 4 * size + 16, size), BF16),
            pltpu.VMEM(b_first.shape, F32),
            pltpu.SemaphoreType.DMA((Y, 5)),
            pltpu.SemaphoreType.DMA((3,)),
        ],
        compiler_params=SMALL,
        name="prologue",
    )(*far(jnp.asarray(forward_rows), activations.reshape(count, channels), w_first, w_second, b_first))
    pieces, act_rows = made[:Y], made[Y]

    weights = []
    for d in range(Y):
        piece = shifted(pieces[d], "y", d) if d else pieces[0]
        weights += [piece, shifted(piece, "core", 1)]
    act_columns = exchange(act_rows)
    turned = pl.pallas_call(
        turn_y_kernel,
        in_specs=[vmem] * 2,
        out_specs=[vmem] * Y,
        out_shape=[shaped(2, X, tile, size)] * Y,
        compiler_params=SMALL,
        name="turn_y",
    )(*near(*arrived))
    arrived = [turned[0]] + [shifted(turned[d], "y", d) for d in range(1, Y)]
    turned = pl.pallas_call(
        turn_x_kernel,
        in_specs=[vmem] * Y,
        out_specs=[vmem] * X,
        out_shape=[shaped(Y, 2, tile, size)] * X,
        compiler_params=SMALL,
        name="turn_x",
    )(*near(*arrived))
    cots = [turned[0]] + [shifted(turned[e], "x", e) for e in range(1, X)]

    tables = [jnp.asarray(table) for table in (forward_columns, inverse_columns, folds)]
    back = pl.pallas_call(
        chain_kernel,
        in_specs=[vmem] * (4 + X) + [hbm] * sections,
        out_specs=vmem,
        out_shape=shaped(*blocks),
        scratch_shapes=[
            pltpu.VMEM((Z, X, tile, size), BF16),
            pltpu.VMEM((sections, 4 * size + 16, size), BF16),
            pltpu.SemaphoreType.DMA((sections,)),
        ],
        compiler_params=TIGHT,
        name="chain",
    )(*near(act_columns, *tables, *cots), *far(*weights))
    grads = pl.pallas_call(
        inverse_kernel,
        in_specs=[vmem] * 3,
        out_specs=hbm,
        out_shape=jax.ShapeDtypeStruct((count, channels), BF16),
        scratch_shapes=[pltpu.VMEM((count, channels), BF16), pltpu.SemaphoreType.DMA((sections,))],
        compiler_params=SMALL,
        name="inverse_rows",
    )(*near(jnp.asarray(inverse_rows), exchange(back), flat_cot))
    return grads.reshape(1, rows, width, channels)


def solution(mesh):
    chips = Mesh(mesh.devices.reshape(Y, 2, X, Z), ("y", "core", "x", "z"))
    pipe, space = ("y", "core"), ("x", "z")
    in_specs = (
        P(pipe, space, None, None),
        P(space, None, None),
        P(pipe, None, None, None, None),
        P(pipe, None, None, None, None),
        P(pipe, None, None),
    )
    out_specs = P(pipe, space, None, None)
    return jax.shard_map(body, mesh=chips, in_specs=in_specs, out_specs=out_specs, check_vma=False)
```

```python
import math

import jax
import jax.numpy as jnp
import numpy as np
from jax import lax
from jax.experimental import pallas as pl
from jax.experimental.pallas import tpu as pltpu
from jax.sharding import Mesh
from jax.sharding import PartitionSpec as P


BF16 = jnp.bfloat16
F32 = jnp.float32
X, Y, Z = 4, 4, 8
SMALL = pltpu.CompilerParams(vmem_limit_bytes=20 << 20)
TIGHT = pltpu.CompilerParams(vmem_limit_bytes=20 << 20)
EVERYONE = ("z", "core", "x", "y")


def two_parts(table):
    high = table.astype(np.float32).astype(BF16)
    low = (table - high.astype(np.float64)).astype(np.float32).astype(BF16)
    return np.concatenate([high, low], axis=1)


def row_matrix(rows, width, columns):
    modes = width // 2
    pair = modes // columns
    angles = 2.0 * math.pi * (np.outer(np.arange(modes), np.arange(width)) % width) / width
    scale = 1.0 / math.sqrt(width)
    parts = np.stack([np.cos(angles), -np.sin(angles)]) * scale
    table = np.zeros((columns, rows, 2, pair, rows, width))
    by_column = parts.reshape(2, columns, pair, width).transpose(1, 0, 2, 3)
    for h in range(rows):
        table[:, h, :, :, h, :] = by_column
    return table.reshape(columns * rows * 2 * pair, rows * width)


def column_matrix(height, pair):
    angles = 2.0 * math.pi * (np.outer(np.arange(height), np.arange(height)) % height) / height
    scale = 1.0 / math.sqrt(height)
    cosines, sines = np.cos(angles) * scale, np.sin(angles) * scale
    table = np.zeros((2, pair, height, height, 2, pair))
    for k in range(pair):
        table[0, k, :, :, 0, k] = cosines
        table[0, k, :, :, 1, k] = sines
        table[1, k, :, :, 1, k] = cosines
        table[1, k, :, :, 0, k] = -sines
    return table.reshape(2 * pair * height, 2 * pair * height)


def fold_matrices(height, pair):
    size = 2 * pair * height
    plain = np.eye(size)
    folded = np.eye(size).reshape(2, pair, height, 2, pair, height)
    eye = np.eye(height)
    flip = eye[(-np.arange(height)) % height]
    folded[0, 0, :, 0, 0, :] = 0.5 * (eye + flip)
    folded[1, 0, :, 1, 0, :] = 0.5 * (eye - flip)
    return np.stack([plain, folded.reshape(size, size)]).astype(np.float32).astype(BF16)


def dot(left, right):
    return jnp.dot(left, right, preferred_element_type=F32)


def dot_t(left, right):
    return lax.dot_general(left, right, (((1,), (1,)), ((), ())), preferred_element_type=F32)


def gelu_slope(values):
    return (
        0.5 * (1.0 + lax.erf(values * 0.7071067811865476))
        + values * jnp.exp(-0.5 * values * values) * 0.3989422804014327
    )


def twice(table_ref, operand):
    depth = operand.shape[0]
    return dot(table_ref[:, :depth], operand) + dot(table_ref[:, depth:], operand)


def first_kernel(table_hbm, act_hbm, cot_hbm, first_ref, second_ref, bias_hbm, *rest):
    pieces, outs, rows_ref = rest[:Y], rest[Y : Y + 2], rest[Y + 2]
    part, field, table_ref, act_ref, held, biases, sems, own_sems = rest[Y + 3 :]
    size = held.shape[2]
    y, core, z, odd = (*(lax.axis_index(name) for name in ("y", "core", "z")), lax.axis_index("x") & 1)
    targets = [(z + y + 4 * i) & (Z - 1) for i in range(2)]
    lines = part.shape[1]
    pairs = [
        (table_hbm.at[pl.ds((targets[0] * 2 + core) * lines, lines)], part.at[0]),
        (table_hbm.at[pl.ds((targets[1] * 2 + core) * lines, lines)], part.at[1]),
        (cot_hbm, field),
        (table_hbm, table_ref),
        (act_hbm, act_ref),
        (bias_hbm, biases),
    ]
    own = []
    for k, (source, target) in enumerate(pairs):
        copy = pltpu.make_async_copy(source, target, own_sems.at[k])
        copy.start()
        own.append(copy)
        if k != 2:
            continue
        loads = []
        for d in range(Y):
            block = ((y + d) & (Y - 1)) * 2 + odd
            for i in range(2):
                for j, ref in enumerate((first_ref, second_ref)):
                    copy = pltpu.make_async_copy(
                        ref.at[0, i, block],
                        held.at[d, pl.ds((2 * j + i) * size, size)],
                        sems.at[d, 2 * j + i],
                    )
                    copy.start()
                    loads.append(copy)

    depth = table_ref.shape[1] // 2
    line = lax.broadcasted_iota(jnp.int32, (lines, size), 0)
    first_even = jnp.logical_and(line < 8, (line & 1) == 0)
    factors = []
    for target in targets:
        zero_mode = jnp.logical_and(first_even, jnp.logical_and(target == 0, core == 0))
        factors.append(jnp.where(zero_mode, 1.0, 2.0).astype(F32))
    for copy in own[:3]:
        copy.wait()
    rows = jnp.concatenate([part[0, :, :depth], part[1, :, :depth], part[0, :, depth:], part[1, :, depth:]], axis=0)
    for n in range(2 * Y):
        spectrum = dot(rows, field[:, n * size : (n + 1) * size])
        spectrum = spectrum[: 2 * lines] + spectrum[2 * lines :]
        for i in range(2):
            tiles = (spectrum[i * lines : (i + 1) * lines] * factors[i]).astype(BF16)
            for m in range(2):
                outs[i][n // 2, 2 * m + n % 2] = tiles[m * 8 : (m + 1) * 8]

    for copy in own[3:]:
        copy.wait()
    for d in range(Y):
        block = ((y + d) & (Y - 1)) * 2 + odd
        bias = biases[0, :, pl.ds(block * size, size)]
        high = bias.astype(BF16).astype(F32)
        middle = (bias - high).astype(BF16).astype(F32)
        low = bias - high - middle
        packed = jnp.concatenate([high, middle, low, jnp.zeros((10, size), F32)], axis=0)
        held[d, 4 * size : 4 * size + 16] = packed.astype(BF16)
    for copy in loads:
        copy.wait()
    stores = []
    for d in range(Y):
        copy = pltpu.make_async_copy(held.at[d], pieces[d], sems.at[d, 4])
        copy.start()
        stores.append(copy)
    for n in range(2 * Y):
        spectrum = twice(table_ref, act_ref[:, n * size : (n + 1) * size]).astype(BF16)
        rows_ref[:, :, :, n % 2, n // 2] = spectrum.reshape(Z, 2, 2, 8, size)
    for copy in stores:
        copy.wait()


def turn_y_kernel(*refs):
    arrived, outs = refs[:2], refs[2:]
    y = lax.axis_index("y")
    for d in range(Y):
        for i in range(2):
            outs[d][i] = arrived[i][(y + d) & (Y - 1)]


def turn_x_kernel(*refs):
    arrived, outs = refs[:Y], refs[Y:]
    x = lax.axis_index("x")
    for e in range(X):
        for d in range(Y):
            outs[e][d] = arrived[d][:, (x + e) & (X - 1)]


def inverse_kernel(table_ref, spec_ref, cot_ref, out_ref, result, sems):
    rows = table_ref.shape[0]
    size = spec_ref.shape[6]
    copies = []
    for n in range(2 * Y):
        block = slice(n * size, (n + 1) * size)
        field = twice(table_ref, spec_ref[:, :, :, n % 2, n // 2].reshape(rows, size))
        result[:, block] = (field + cot_ref[:, block].astype(F32)).astype(BF16)
        copy = pltpu.make_async_copy(result.at[:, block], out_ref.at[:, block], sems.at[n])
        copy.start()
        copies.append(copy)
    for copy in copies:
        copy.wait()


def chain_kernel(act_ref, col_ref, inv_ref, fold_ref, *rest):
    sections = 2 * Y
    cots, weights = rest[:X], rest[X : X + sections]
    out_ref, found, held, sems = rest[X + sections :]
    size = act_ref.shape[6]
    half = col_ref.shape[0] // 2
    y, core, x, z = (lax.axis_index(name) for name in ("y", "core", "x", "z"))

    def load(p, source):
        return pltpu.make_async_copy(weights[source], held.at[p], sems.at[p])

    for here in range(sections):

        @pl.when(y * 2 + core == here)
        def _():
            for p in range(sections - 1, -1, -1):
                load(p, 2 * ((here // 2 - p // 2) % Y) + (p % 2 != here % 2)).start()

    for e in range(X):
        for d in range(Y):
            for i in range(2):
                found[(z - ((y - d) & (Y - 1)) - 4 * i) & (Z - 1), (x - e) & (X - 1)] = cots[e][d, i]
    has_zero = jnp.logical_and(jnp.logical_and(core == 0, x < 2), z == 0)
    fold = jnp.where(has_zero, 1, 0)

    base = twice(col_ref, found[...].reshape(2 * half, size))
    total = jnp.zeros_like(base)
    height_total = jnp.zeros_like(base)
    grad = base.astype(BF16)
    spectra = []
    for p in range(sections):
        columns = act_ref[:, p % 2, :, :, p // 2].reshape(2 * half, size)
        spectra.append(twice(col_ref, columns).astype(BF16))

    for p in range(sections - 1, -1, -1):
        load(p, 0).wait()
        a_re, a_im = held[p, 0:size], held[p, size : 2 * size]
        b_re, b_im = held[p, 2 * size : 3 * size], held[p, 3 * size : 4 * size]
        bias = held[p, 4 * size : 4 * size + 16].astype(F32)
        bias_re = bias[0:1] + bias[2:3] + bias[4:5]
        bias_im = bias[1:2] + bias[3:4] + bias[5:6]
        s = spectra[p]
        s_turned = jnp.concatenate([-s[half:], s[:half]], axis=0)
        z_both = dot(s, a_re) + dot(s_turned, a_im)
        slope = gelu_slope(jnp.concatenate([z_both[:half] + bias_re, z_both[half:] + bias_im], axis=0))
        g_turned = jnp.concatenate([grad[half:], -grad[:half]], axis=0)
        u = dot_t(grad, b_re) + dot_t(g_turned, b_im)
        q = (u * slope).astype(BF16)
        q_turned = jnp.concatenate([q[half:], -q[:half]], axis=0)
        e = (dot_t(q, a_re) + dot_t(q_turned, a_im)).astype(BF16)
        height_total = height_total + twice(inv_ref, e)
        out_ref[:, p % 2, :, :, p // 2] = height_total.astype(BF16).reshape(Z, 2, 2, 8, size)
        if p > 0:
            total = total + dot(fold_ref[fold], e)
            grad = (base + total).astype(BF16)


def body(activations, cotangent, w_first, w_second, b_first):
    sections, columns = 2 * Y, X * Z
    _, rows, width, channels = activations.shape
    size = w_first.shape[3]
    height = rows * columns
    pair = width // 2 // columns
    count = rows * width
    tile = 2 * rows * pair
    row_table = row_matrix(rows, width, columns)
    row_table = row_table.reshape(2, 2, Z, -1).transpose(2, 0, 1, 3).reshape(row_table.shape)
    forward_rows, inverse_rows = two_parts(row_table), two_parts(row_table.T)
    column_table = column_matrix(height, pair)
    column_table = column_table.reshape(-1, X, Z, tile).transpose(0, 2, 1, 3).reshape(column_table.shape)
    forward_columns, inverse_columns = two_parts(column_table), two_parts(column_table.T)
    folds = fold_matrices(height, pair)

    vmem = pl.BlockSpec(memory_space=pltpu.VMEM)
    hbm = pl.BlockSpec(memory_space=pl.ANY)
    blocks = (Z, 2, 2, 2, Y, tile, size)

    def shaped(*dims):
        return pltpu.VMEM(dims, BF16)

    def near(*values):
        return [pltpu.with_memory_space_constraint(value, pltpu.VMEM) for value in values]

    def far(*values):
        return [pltpu.with_memory_space_constraint(value, pltpu.HBM) for value in values]

    def exchange(value):
        flat = value.reshape(sections * columns, tile, size)
        return lax.all_to_all(flat, EVERYONE, split_axis=0, concat_axis=0, tiled=True).reshape(blocks)

    def shifted(value, axis, distance):
        size = lax.axis_size(axis)
        return lax.ppermute(value, axis, [(i, (i + distance) % size) for i in range(size)])

    flat_cot = cotangent.reshape(count, channels)
    made = pl.pallas_call(
        first_kernel,
        in_specs=[hbm] * 6,
        out_specs=[hbm] * Y + [vmem] * 3,
        out_shape=[pltpu.HBM((4 * size + 16, size), BF16)] * Y
        + [shaped(Y, X, tile, size)] * 2
        + [shaped(*blocks)],
        scratch_shapes=[
            pltpu.VMEM((2, 2 * tile, 2 * count), BF16),
            pltpu.VMEM((count, channels), BF16),
            pltpu.VMEM(forward_rows.shape, BF16),
            pltpu.VMEM((count, channels), BF16),
            pltpu.VMEM((Y, 4 * size + 16, size), BF16),
            pltpu.VMEM(b_first.shape, F32),
            pltpu.SemaphoreType.DMA((Y, 5)),
            pltpu.SemaphoreType.DMA((6,)),
        ],
        compiler_params=SMALL,
        name="first",
    )(
        *far(
            jnp.asarray(forward_rows),
            activations.reshape(count, channels),
            flat_cot,
            w_first,
            w_second,
            b_first,
        )
    )
    pieces, cot_rows, act_rows = made[:Y], made[Y : Y + 2], made[Y + 2]
    arrived = []
    for i in range(2):
        route = [(y * Z + z, y * Z + (z + y + 4 * i) % Z) for y in range(Y) for z in range(Z)]
        arrived.append(lax.ppermute(cot_rows[i], ("y", "z"), route))
    weights = []
    for d in range(Y):
        piece = shifted(pieces[d], "y", d) if d else pieces[0]
        weights += [piece, shifted(piece, "core", 1)]
    act_columns = exchange(act_rows)
    turned = pl.pallas_call(
        turn_y_kernel,
        in_specs=[vmem] * 2,
        out_specs=[vmem] * Y,
        out_shape=[shaped(2, X, tile, size)] * Y,
        compiler_params=SMALL,
        name="turn_y",
    )(*near(*arrived))
    arrived = [turned[0]] + [shifted(turned[d], "y", d) for d in range(1, Y)]
    turned = pl.pallas_call(
        turn_x_kernel,
        in_specs=[vmem] * Y,
        out_specs=[vmem] * X,
        out_shape=[shaped(Y, 2, tile, size)] * X,
        compiler_params=SMALL,
        name="turn_x",
    )(*near(*arrived))
    cots = [turned[0]] + [shifted(turned[e], "x", e) for e in range(1, X)]

    tables = [jnp.asarray(table) for table in (forward_columns, inverse_columns, folds)]
    back = pl.pallas_call(
        chain_kernel,
        in_specs=[vmem] * (4 + X) + [hbm] * sections,
        out_specs=vmem,
        out_shape=shaped(*blocks),
        scratch_shapes=[
            pltpu.VMEM((Z, X, tile, size), BF16),
            pltpu.VMEM((sections, 4 * size + 16, size), BF16),
            pltpu.SemaphoreType.DMA((sections,)),
        ],
        compiler_params=TIGHT,
        name="chain",
    )(*near(act_columns, *tables, *cots), *far(*weights))
    grads = pl.pallas_call(
        inverse_kernel,
        in_specs=[vmem] * 3,
        out_specs=hbm,
        out_shape=jax.ShapeDtypeStruct((count, channels), BF16),
        scratch_shapes=[pltpu.VMEM((count, channels), BF16), pltpu.SemaphoreType.DMA((sections,))],
        compiler_params=SMALL,
        name="inverse_rows",
    )(*near(jnp.asarray(inverse_rows), exchange(back), flat_cot))
    return grads.reshape(1, rows, width, channels)


def solution(mesh):
    chips = Mesh(mesh.devices.reshape(Y, 2, X, Z), ("y", "core", "x", "z"))
    pipe, space = ("y", "core"), ("x", "z")
    in_specs = (
        P(pipe, space, None, None),
        P(space, None, None),
        P(pipe, None, None, None, None),
        P(pipe, None, None, None, None),
        P(pipe, None, None),
    )
    out_specs = P(pipe, space, None, None)
    return jax.shard_map(body, mesh=chips, in_specs=in_specs, out_specs=out_specs, check_vma=False)
```

```python
import math

import jax
import jax.numpy as jnp
import numpy as np
from jax import lax
from jax.experimental import pallas as pl
from jax.experimental.pallas import tpu as pltpu
from jax.sharding import Mesh
from jax.sharding import PartitionSpec as P


BF16 = jnp.bfloat16
F32 = jnp.float32
X, Y, Z = 4, 4, 8
SMALL = pltpu.CompilerParams(vmem_limit_bytes=20 << 20)
TIGHT = pltpu.CompilerParams(vmem_limit_bytes=20 << 20)
EVERYONE = ("z", "core", "x", "y")


def two_parts(table):
    high = table.astype(np.float32).astype(BF16)
    low = (table - high.astype(np.float64)).astype(np.float32).astype(BF16)
    return np.concatenate([high, low], axis=1)


def row_matrix(rows, width, columns):
    modes = width // 2
    pair = modes // columns
    angles = 2.0 * math.pi * (np.outer(np.arange(modes), np.arange(width)) % width) / width
    scale = 1.0 / math.sqrt(width)
    parts = np.stack([np.cos(angles), -np.sin(angles)]) * scale
    table = np.zeros((columns, rows, 2, pair, rows, width))
    by_column = parts.reshape(2, columns, pair, width).transpose(1, 0, 2, 3)
    for h in range(rows):
        table[:, h, :, :, h, :] = by_column
    return table.reshape(columns * rows * 2 * pair, rows * width)


def column_matrix(height, pair):
    angles = 2.0 * math.pi * (np.outer(np.arange(height), np.arange(height)) % height) / height
    scale = 1.0 / math.sqrt(height)
    cosines, sines = np.cos(angles) * scale, np.sin(angles) * scale
    table = np.zeros((2, pair, height, height, 2, pair))
    for k in range(pair):
        table[0, k, :, :, 0, k] = cosines
        table[0, k, :, :, 1, k] = sines
        table[1, k, :, :, 1, k] = cosines
        table[1, k, :, :, 0, k] = -sines
    return table.reshape(2 * pair * height, 2 * pair * height)


def fold_matrices(height, pair):
    size = 2 * pair * height
    plain = np.eye(size)
    folded = np.eye(size).reshape(2, pair, height, 2, pair, height)
    eye = np.eye(height)
    flip = eye[(-np.arange(height)) % height]
    folded[0, 0, :, 0, 0, :] = 0.5 * (eye + flip)
    folded[1, 0, :, 1, 0, :] = 0.5 * (eye - flip)
    return np.stack([plain, folded.reshape(size, size)]).astype(np.float32).astype(BF16)


def dot(left, right):
    return jnp.dot(left, right, preferred_element_type=F32)


def dot_t(left, right):
    return lax.dot_general(left, right, (((1,), (1,)), ((), ())), preferred_element_type=F32)


def gelu_slope(values):
    return (
        0.5 * (1.0 + lax.erf(values * 0.7071067811865476))
        + values * jnp.exp(-0.5 * values * values) * 0.3989422804014327
    )


def twice(table_ref, operand):
    depth = operand.shape[0]
    return dot(table_ref[:, :depth], operand) + dot(table_ref[:, depth:], operand)


def first_kernel(table_hbm, act_hbm, cot_hbm, first_ref, second_ref, bias_hbm, *rest):
    pieces, cot_rows_ref, rows_ref = rest[:Y], rest[Y], rest[Y + 1]
    part, field, table_ref, act_ref, held, biases, sems, own_sems = rest[Y + 2 :]
    size = held.shape[2]
    y, core, z, odd = (*(lax.axis_index(name) for name in ("y", "core", "z")), lax.axis_index("x") & 1)
    target = (z + y + 4 * core) & (Z - 1)
    lines = part.shape[0]
    pairs = [
        (table_hbm.at[pl.ds(target * lines, lines)], part),
        (cot_hbm, field),
        (table_hbm, table_ref),
        (act_hbm, act_ref),
        (bias_hbm, biases),
    ]
    own = []
    for k, (source, place) in enumerate(pairs):
        copy = pltpu.make_async_copy(source, place, own_sems.at[k])
        copy.start()
        own.append(copy)
        if k != 1:
            continue
        loads = []
        for d in range(Y):
            block = ((y + d) & (Y - 1)) * 2 + odd
            for i in range(2):
                for j, ref in enumerate((first_ref, second_ref)):
                    copy = pltpu.make_async_copy(
                        ref.at[0, i, block],
                        held.at[d, pl.ds((2 * j + i) * size, size)],
                        sems.at[d, 2 * j + i],
                    )
                    copy.start()
                    loads.append(copy)

    depth = table_ref.shape[1] // 2
    line = lax.broadcasted_iota(jnp.int32, (lines, size), 0)
    zero_mode = jnp.logical_and(jnp.logical_and(line < 8, (line & 1) == 0), target == 0)
    factor = jnp.where(zero_mode, 1.0, 2.0).astype(F32)
    for copy in own[:2]:
        copy.wait()
    rows = jnp.concatenate([part[:, :depth], part[:, depth:]], axis=0)
    for n in range(2 * Y):
        spectrum = dot(rows, field[:, n * size : (n + 1) * size])
        tiles = ((spectrum[:lines] + spectrum[lines:]) * factor).astype(BF16)
        for i in range(2):
            for m in range(2):
                cot_rows_ref[i, n // 2, 2 * m + n % 2] = tiles[(2 * i + m) * 8 : (2 * i + m + 1) * 8]

    for copy in own[2:]:
        copy.wait()
    for d in range(Y):
        block = ((y + d) & (Y - 1)) * 2 + odd
        bias = biases[0, :, pl.ds(block * size, size)]
        high = bias.astype(BF16).astype(F32)
        middle = (bias - high).astype(BF16).astype(F32)
        low = bias - high - middle
        packed = jnp.concatenate([high, middle, low, jnp.zeros((10, size), F32)], axis=0)
        held[d, 4 * size : 4 * size + 16] = packed.astype(BF16)
    for copy in loads:
        copy.wait()
    stores = []
    for d in range(Y):
        copy = pltpu.make_async_copy(held.at[d], pieces[d], sems.at[d, 4])
        copy.start()
        stores.append(copy)
    for n in range(2 * Y):
        spectrum = twice(table_ref, act_ref[:, n * size : (n + 1) * size]).astype(BF16)
        rows_ref[:, :, :, n % 2, n // 2] = spectrum.reshape(Z, 2, 2, 8, size)
    for copy in stores:
        copy.wait()


def turn_core_kernel(arrived_ref, kept_ref, sent_ref):
    core = lax.axis_index("core")
    kept_ref[...] = arrived_ref[core]
    sent_ref[...] = arrived_ref[1 - core]


def turn_y_kernel(kept_ref, arrived_ref, *outs):
    y, core = lax.axis_index("y"), lax.axis_index("core")
    for d in range(Y):
        to = (y + d) & (Y - 1)
        outs[d][core] = kept_ref[to]
        outs[d][1 - core] = arrived_ref[to]


def turn_x_kernel(*refs):
    arrived, outs = refs[:Y], refs[Y:]
    x = lax.axis_index("x")
    for e in range(X):
        for d in range(Y):
            outs[e][d] = arrived[d][:, (x + e) & (X - 1)]


def inverse_kernel(table_ref, spec_ref, cot_ref, out_ref, result, sems):
    rows = table_ref.shape[0]
    size = spec_ref.shape[6]
    copies = []
    for n in range(2 * Y):
        block = slice(n * size, (n + 1) * size)
        field = twice(table_ref, spec_ref[:, :, :, n % 2, n // 2].reshape(rows, size))
        result[:, block] = (field + cot_ref[:, block].astype(F32)).astype(BF16)
        copy = pltpu.make_async_copy(result.at[:, block], out_ref.at[:, block], sems.at[n])
        copy.start()
        copies.append(copy)
    for copy in copies:
        copy.wait()


def chain_kernel(act_ref, col_ref, inv_ref, fold_ref, *rest):
    sections = 2 * Y
    cots, weights = rest[:X], rest[X : X + sections]
    out_ref, found, held, sems = rest[X + sections :]
    size = act_ref.shape[6]
    half = col_ref.shape[0] // 2
    y, core, x, z = (lax.axis_index(name) for name in ("y", "core", "x", "z"))

    def load(p, source):
        return pltpu.make_async_copy(weights[source], held.at[p], sems.at[p])

    for here in range(sections):

        @pl.when(y * 2 + core == here)
        def _():
            for p in range(sections - 1, -1, -1):
                load(p, 2 * ((here // 2 - p // 2) % Y) + (p % 2 != here % 2)).start()

    for e in range(X):
        for d in range(Y):
            for i in range(2):
                found[(z - ((y - d) & (Y - 1)) - 4 * i) & (Z - 1), (x - e) & (X - 1)] = cots[e][d, i]
    has_zero = jnp.logical_and(jnp.logical_and(core == 0, x < 2), z == 0)
    fold = jnp.where(has_zero, 1, 0)

    base = twice(col_ref, found[...].reshape(2 * half, size))
    total = jnp.zeros_like(base)
    height_total = jnp.zeros_like(base)
    grad = base.astype(BF16)
    spectra = []
    for p in range(sections):
        columns = act_ref[:, p % 2, :, :, p // 2].reshape(2 * half, size)
        spectra.append(twice(col_ref, columns).astype(BF16))

    for p in range(sections - 1, -1, -1):
        load(p, 0).wait()
        a_re, a_im = held[p, 0:size], held[p, size : 2 * size]
        b_re, b_im = held[p, 2 * size : 3 * size], held[p, 3 * size : 4 * size]
        bias = held[p, 4 * size : 4 * size + 16].astype(F32)
        bias_re = bias[0:1] + bias[2:3] + bias[4:5]
        bias_im = bias[1:2] + bias[3:4] + bias[5:6]
        s = spectra[p]
        s_turned = jnp.concatenate([-s[half:], s[:half]], axis=0)
        z_both = dot(s, a_re) + dot(s_turned, a_im)
        slope = gelu_slope(jnp.concatenate([z_both[:half] + bias_re, z_both[half:] + bias_im], axis=0))
        g_turned = jnp.concatenate([grad[half:], -grad[:half]], axis=0)
        u = dot_t(grad, b_re) + dot_t(g_turned, b_im)
        q = (u * slope).astype(BF16)
        q_turned = jnp.concatenate([q[half:], -q[:half]], axis=0)
        e = (dot_t(q, a_re) + dot_t(q_turned, a_im)).astype(BF16)
        height_total = height_total + twice(inv_ref, e)
        out_ref[:, p % 2, :, :, p // 2] = height_total.astype(BF16).reshape(Z, 2, 2, 8, size)
        if p > 0:
            total = total + dot(fold_ref[fold], e)
            grad = (base + total).astype(BF16)


def body(activations, cotangent, w_first, w_second, b_first):
    sections, columns = 2 * Y, X * Z
    _, rows, width, channels = activations.shape
    size = w_first.shape[3]
    height = rows * columns
    pair = width // 2 // columns
    count = rows * width
    tile = 2 * rows * pair
    row_table = row_matrix(rows, width, columns)
    row_table = row_table.reshape(2, 2, Z, -1).transpose(2, 0, 1, 3).reshape(row_table.shape)
    forward_rows, inverse_rows = two_parts(row_table), two_parts(row_table.T)
    column_table = column_matrix(height, pair)
    column_table = column_table.reshape(-1, X, Z, tile).transpose(0, 2, 1, 3).reshape(column_table.shape)
    forward_columns, inverse_columns = two_parts(column_table), two_parts(column_table.T)
    folds = fold_matrices(height, pair)

    vmem = pl.BlockSpec(memory_space=pltpu.VMEM)
    hbm = pl.BlockSpec(memory_space=pl.ANY)
    blocks = (Z, 2, 2, 2, Y, tile, size)

    def shaped(*dims):
        return pltpu.VMEM(dims, BF16)

    def near(*values):
        return [pltpu.with_memory_space_constraint(value, pltpu.VMEM) for value in values]

    def far(*values):
        return [pltpu.with_memory_space_constraint(value, pltpu.HBM) for value in values]

    def exchange(value):
        flat = value.reshape(sections * columns, tile, size)
        return lax.all_to_all(flat, EVERYONE, split_axis=0, concat_axis=0, tiled=True).reshape(blocks)

    def shifted(value, axis, distance):
        size = lax.axis_size(axis)
        return lax.ppermute(value, axis, [(i, (i + distance) % size) for i in range(size)])

    flat_cot = cotangent.reshape(count, channels)
    made = pl.pallas_call(
        first_kernel,
        in_specs=[hbm] * 6,
        out_specs=[hbm] * Y + [vmem] * 2,
        out_shape=[pltpu.HBM((4 * size + 16, size), BF16)] * Y + [shaped(2, Y, X, tile, size), shaped(*blocks)],
        scratch_shapes=[
            pltpu.VMEM((4 * tile, 2 * count), BF16),
            pltpu.VMEM((count, channels), BF16),
            pltpu.VMEM(forward_rows.shape, BF16),
            pltpu.VMEM((count, channels), BF16),
            pltpu.VMEM((Y, 4 * size + 16, size), BF16),
            pltpu.VMEM(b_first.shape, F32),
            pltpu.SemaphoreType.DMA((Y, 5)),
            pltpu.SemaphoreType.DMA((5,)),
        ],
        compiler_params=SMALL,
        name="first",
    )(
        *far(
            jnp.asarray(forward_rows),
            activations.reshape(count, channels),
            flat_cot,
            w_first,
            w_second,
            b_first,
        )
    )
    pieces, cot_rows, act_rows = made[:Y], made[Y], made[Y + 1]
    route = []
    for line in range(2 * Y):
        shift = line // 2 + 4 * (line % 2)
        route += [(line * Z + z, line * Z + (z + shift) % Z) for z in range(Z)]
    arrived = lax.ppermute(cot_rows, ("y", "core", "z"), route)
    weights = []
    for d in range(Y):
        piece = shifted(pieces[d], "y", d) if d else pieces[0]
        weights += [piece, shifted(piece, "core", 1)]
    act_columns = exchange(act_rows)
    kept, sent = pl.pallas_call(
        turn_core_kernel,
        in_specs=[vmem],
        out_specs=[vmem] * 2,
        out_shape=[shaped(Y, X, tile, size)] * 2,
        compiler_params=SMALL,
        name="turn_core",
    )(*near(arrived))
    arrived = shifted(sent, "core", 1)
    turned = pl.pallas_call(
        turn_y_kernel,
        in_specs=[vmem] * 2,
        out_specs=[vmem] * Y,
        out_shape=[shaped(2, X, tile, size)] * Y,
        compiler_params=SMALL,
        name="turn_y",
    )(*near(kept, arrived))
    arrived = [turned[0]] + [shifted(turned[d], "y", d) for d in range(1, Y)]
    turned = pl.pallas_call(
        turn_x_kernel,
        in_specs=[vmem] * Y,
        out_specs=[vmem] * X,
        out_shape=[shaped(Y, 2, tile, size)] * X,
        compiler_params=SMALL,
        name="turn_x",
    )(*near(*arrived))
    cots = [turned[0]] + [shifted(turned[e], "x", e) for e in range(1, X)]

    tables = [jnp.asarray(table) for table in (forward_columns, inverse_columns, folds)]
    back = pl.pallas_call(
        chain_kernel,
        in_specs=[vmem] * (4 + X) + [hbm] * sections,
        out_specs=vmem,
        out_shape=shaped(*blocks),
        scratch_shapes=[
            pltpu.VMEM((Z, X, tile, size), BF16),
            pltpu.VMEM((sections, 4 * size + 16, size), BF16),
            pltpu.SemaphoreType.DMA((sections,)),
        ],
        compiler_params=TIGHT,
        name="chain",
    )(*near(act_columns, *tables, *cots), *far(*weights))
    grads = pl.pallas_call(
        inverse_kernel,
        in_specs=[vmem] * 3,
        out_specs=hbm,
        out_shape=jax.ShapeDtypeStruct((count, channels), BF16),
        scratch_shapes=[pltpu.VMEM((count, channels), BF16), pltpu.SemaphoreType.DMA((sections,))],
        compiler_params=SMALL,
        name="inverse_rows",
    )(*near(jnp.asarray(inverse_rows), exchange(back), flat_cot))
    return grads.reshape(1, rows, width, channels)


def solution(mesh):
    chips = Mesh(mesh.devices.reshape(Y, 2, X, Z), ("y", "core", "x", "z"))
    pipe, space = ("y", "core"), ("x", "z")
    in_specs = (
        P(pipe, space, None, None),
        P(space, None, None),
        P(pipe, None, None, None, None),
        P(pipe, None, None, None, None),
        P(pipe, None, None),
    )
    out_specs = P(pipe, space, None, None)
    return jax.shard_map(body, mesh=chips, in_specs=in_specs, out_specs=out_specs, check_vma=False)
```

```python
import math

import jax
import jax.numpy as jnp
import numpy as np
from jax import lax
from jax.experimental import pallas as pl
from jax.experimental.pallas import tpu as pltpu
from jax.sharding import Mesh
from jax.sharding import PartitionSpec as P


BF16 = jnp.bfloat16
F32 = jnp.float32
X, Y, Z = 4, 4, 8
SMALL = pltpu.CompilerParams(vmem_limit_bytes=20 << 20)
TIGHT = pltpu.CompilerParams(vmem_limit_bytes=20 << 20)
EVERYONE = ("z", "core", "x", "y")


def rounded(table):
    return table.astype(np.float32).astype(BF16)


def row_matrix(rows, width, columns):
    modes = width // 2
    pair = modes // columns
    angles = 2.0 * math.pi * (np.outer(np.arange(modes), np.arange(width)) % width) / width
    scale = 1.0 / math.sqrt(width)
    parts = np.stack([np.cos(angles), -np.sin(angles)]) * scale
    table = np.zeros((columns, rows, 2, pair, rows, width))
    by_column = parts.reshape(2, columns, pair, width).transpose(1, 0, 2, 3)
    for h in range(rows):
        table[:, h, :, :, h, :] = by_column
    return table.reshape(columns * rows * 2 * pair, rows * width)


def column_matrix(height, pair):
    angles = 2.0 * math.pi * (np.outer(np.arange(height), np.arange(height)) % height) / height
    scale = 1.0 / math.sqrt(height)
    cosines, sines = np.cos(angles) * scale, np.sin(angles) * scale
    table = np.zeros((2, pair, height, height, 2, pair))
    for k in range(pair):
        table[0, k, :, :, 0, k] = cosines
        table[0, k, :, :, 1, k] = sines
        table[1, k, :, :, 1, k] = cosines
        table[1, k, :, :, 0, k] = -sines
    return table.reshape(2 * pair * height, 2 * pair * height)


def fold_matrices(height, pair):
    size = 2 * pair * height
    plain = np.eye(size)
    folded = np.eye(size).reshape(2, pair, height, 2, pair, height)
    eye = np.eye(height)
    flip = eye[(-np.arange(height)) % height]
    folded[0, 0, :, 0, 0, :] = 0.5 * (eye + flip)
    folded[1, 0, :, 1, 0, :] = 0.5 * (eye - flip)
    return np.stack([plain, folded.reshape(size, size)]).astype(np.float32).astype(BF16)


def dot(left, right):
    return jnp.dot(left, right, preferred_element_type=F32)


def dot_t(left, right):
    return lax.dot_general(left, right, (((1,), (1,)), ((), ())), preferred_element_type=F32)


def gelu_slope(values):
    return (
        0.5 * (1.0 + lax.erf(values * 0.7071067811865476))
        + values * jnp.exp(-0.5 * values * values) * 0.3989422804014327
    )


def first_kernel(table_hbm, act_hbm, cot_hbm, first_ref, second_ref, bias_hbm, *rest):
    pieces, cot_rows_ref, rows_ref = rest[:Y], rest[Y], rest[Y + 1]
    part, field, table_ref, act_ref, held, biases, sems, own_sems = rest[Y + 2 :]
    size = held.shape[2]
    y, core, z, odd = (*(lax.axis_index(name) for name in ("y", "core", "z")), lax.axis_index("x") & 1)
    target = (z + y + 4 * core) & (Z - 1)
    lines = part.shape[0]
    pairs = [
        (table_hbm.at[pl.ds(target * lines, lines)], part),
        (cot_hbm, field),
        (table_hbm, table_ref),
        (act_hbm, act_ref),
        (bias_hbm, biases),
    ]
    own = []
    for k, (source, place) in enumerate(pairs):
        copy = pltpu.make_async_copy(source, place, own_sems.at[k])
        copy.start()
        own.append(copy)
        if k != 1:
            continue
        loads = []
        for d in range(Y):
            block = ((y + d) & (Y - 1)) * 2 + odd
            for i in range(2):
                for j, ref in enumerate((first_ref, second_ref)):
                    copy = pltpu.make_async_copy(
                        ref.at[0, i, block],
                        held.at[d, pl.ds((2 * j + i) * size, size)],
                        sems.at[d, 2 * j + i],
                    )
                    copy.start()
                    loads.append(copy)

    line = lax.broadcasted_iota(jnp.int32, (lines, size), 0)
    zero_mode = jnp.logical_and(jnp.logical_and(line < 8, (line & 1) == 0), target == 0)
    factor = jnp.where(zero_mode, 1.0, 2.0).astype(F32)
    for copy in own[:2]:
        copy.wait()
    for n in range(2 * Y):
        tiles = (dot(part[...], field[:, n * size : (n + 1) * size]) * factor).astype(BF16)
        for i in range(2):
            for m in range(2):
                cot_rows_ref[i, n // 2, 2 * m + n % 2] = tiles[(2 * i + m) * 8 : (2 * i + m + 1) * 8]

    for copy in own[2:]:
        copy.wait()
    for d in range(Y):
        block = ((y + d) & (Y - 1)) * 2 + odd
        bias = biases[0, :, pl.ds(block * size, size)]
        high = bias.astype(BF16).astype(F32)
        middle = (bias - high).astype(BF16).astype(F32)
        low = bias - high - middle
        packed = jnp.concatenate([high, middle, low, jnp.zeros((10, size), F32)], axis=0)
        held[d, 4 * size : 4 * size + 16] = packed.astype(BF16)
    for copy in loads:
        copy.wait()
    stores = []
    for d in range(Y):
        copy = pltpu.make_async_copy(held.at[d], pieces[d], sems.at[d, 4])
        copy.start()
        stores.append(copy)
    for n in range(2 * Y):
        spectrum = dot(table_ref[...], act_ref[:, n * size : (n + 1) * size]).astype(BF16)
        rows_ref[:, :, :, n % 2, n // 2] = spectrum.reshape(Z, 2, 2, 8, size)
    for copy in stores:
        copy.wait()


def turn_core_kernel(arrived_ref, kept_ref, sent_ref):
    core = lax.axis_index("core")
    kept_ref[...] = arrived_ref[core]
    sent_ref[...] = arrived_ref[1 - core]


def turn_x_kernel(kept_ref, arrived_ref, *outs):
    x, core = lax.axis_index("x"), lax.axis_index("core")
    for e in range(X):
        to = (x + e) & (X - 1)
        outs[e][core] = kept_ref[:, to]
        outs[e][1 - core] = arrived_ref[:, to]


def turn_y_kernel(*refs):
    arrived, outs = refs[:X], refs[X:]
    y = lax.axis_index("y")
    for d in range(Y):
        for e in range(X):
            outs[d][e] = arrived[e][:, (y + d) & (Y - 1)]


def inverse_kernel(table_ref, spec_ref, cot_ref, out_ref, result, sems):
    rows = table_ref.shape[0]
    size = spec_ref.shape[6]
    copies = []
    for n in range(2 * Y):
        block = slice(n * size, (n + 1) * size)
        field = dot(table_ref[...], spec_ref[:, :, :, n % 2, n // 2].reshape(rows, size))
        result[:, block] = (field + cot_ref[:, block].astype(F32)).astype(BF16)
        copy = pltpu.make_async_copy(result.at[:, block], out_ref.at[:, block], sems.at[n])
        copy.start()
        copies.append(copy)
    for copy in copies:
        copy.wait()


def chain_kernel(act_ref, col_ref, inv_ref, fold_ref, *rest):
    sections = 2 * Y
    cots, weights = rest[:X], rest[X : X + sections]
    out_ref, found, held, sems = rest[X + sections :]
    size = act_ref.shape[6]
    half = col_ref.shape[0] // 2
    y, core, x, z = (lax.axis_index(name) for name in ("y", "core", "x", "z"))

    def load(p, source):
        return pltpu.make_async_copy(weights[source], held.at[p], sems.at[p])

    for here in range(sections):

        @pl.when(y * 2 + core == here)
        def _():
            for p in range(sections - 1, -1, -1):
                load(p, 2 * ((here // 2 - p // 2) % Y) + (p % 2 != here % 2)).start()

    for d in range(Y):
        for e in range(X):
            for i in range(2):
                found[(z - ((y - d) & (Y - 1)) - 4 * i) & (Z - 1), (x - e) & (X - 1)] = cots[d][e, i]
    has_zero = jnp.logical_and(jnp.logical_and(core == 0, x < 2), z == 0)
    fold = jnp.where(has_zero, 1, 0)

    base = dot(col_ref[...], found[...].reshape(2 * half, size))
    total = jnp.zeros_like(base)
    height_total = jnp.zeros_like(base)
    grad = base.astype(BF16)
    spectra = []
    for p in range(sections):
        columns = act_ref[:, p % 2, :, :, p // 2].reshape(2 * half, size)
        spectra.append(dot(col_ref[...], columns).astype(BF16))

    for p in range(sections - 1, -1, -1):
        load(p, 0).wait()
        a_re, a_im = held[p, 0:size], held[p, size : 2 * size]
        b_re, b_im = held[p, 2 * size : 3 * size], held[p, 3 * size : 4 * size]
        bias = held[p, 4 * size : 4 * size + 16].astype(F32)
        bias_re = bias[0:1] + bias[2:3] + bias[4:5]
        bias_im = bias[1:2] + bias[3:4] + bias[5:6]
        s = spectra[p]
        s_turned = jnp.concatenate([-s[half:], s[:half]], axis=0)
        z_both = dot(s, a_re) + dot(s_turned, a_im)
        slope = gelu_slope(jnp.concatenate([z_both[:half] + bias_re, z_both[half:] + bias_im], axis=0))
        g_turned = jnp.concatenate([grad[half:], -grad[:half]], axis=0)
        u = dot_t(grad, b_re) + dot_t(g_turned, b_im)
        q = (u * slope).astype(BF16)
        q_turned = jnp.concatenate([q[half:], -q[:half]], axis=0)
        e = (dot_t(q, a_re) + dot_t(q_turned, a_im)).astype(BF16)
        height_total = height_total + dot(inv_ref[...], e)
        out_ref[:, p % 2, :, :, p // 2] = height_total.astype(BF16).reshape(Z, 2, 2, 8, size)
        if p > 0:
            total = total + dot(fold_ref[fold], e)
            grad = (base + total).astype(BF16)


def body(activations, cotangent, w_first, w_second, b_first):
    sections, columns = 2 * Y, X * Z
    _, rows, width, channels = activations.shape
    size = w_first.shape[3]
    height = rows * columns
    pair = width // 2 // columns
    count = rows * width
    tile = 2 * rows * pair
    row_table = row_matrix(rows, width, columns)
    row_table = row_table.reshape(2, 2, Z, -1).transpose(2, 0, 1, 3).reshape(row_table.shape)
    forward_rows, inverse_rows = rounded(row_table), rounded(row_table.T)
    column_table = column_matrix(height, pair)
    column_table = column_table.reshape(-1, X, Z, tile).transpose(0, 2, 1, 3).reshape(column_table.shape)
    forward_columns, inverse_columns = rounded(column_table), rounded(column_table.T)
    folds = fold_matrices(height, pair)

    vmem = pl.BlockSpec(memory_space=pltpu.VMEM)
    hbm = pl.BlockSpec(memory_space=pl.ANY)
    blocks = (Z, 2, 2, 2, Y, tile, size)

    def shaped(*dims):
        return pltpu.VMEM(dims, BF16)

    def near(*values):
        return [pltpu.with_memory_space_constraint(value, pltpu.VMEM) for value in values]

    def far(*values):
        return [pltpu.with_memory_space_constraint(value, pltpu.HBM) for value in values]

    def exchange(value):
        flat = value.reshape(sections * columns, tile, size)
        return lax.all_to_all(flat, EVERYONE, split_axis=0, concat_axis=0, tiled=True).reshape(blocks)

    def shifted(value, axis, distance):
        size = lax.axis_size(axis)
        return lax.ppermute(value, axis, [(i, (i + distance) % size) for i in range(size)])

    flat_cot = cotangent.reshape(count, channels)
    made = pl.pallas_call(
        first_kernel,
        in_specs=[hbm] * 6,
        out_specs=[hbm] * Y + [vmem] * 2,
        out_shape=[pltpu.HBM((4 * size + 16, size), BF16)] * Y + [shaped(2, Y, X, tile, size), shaped(*blocks)],
        scratch_shapes=[
            pltpu.VMEM((4 * tile, count), BF16),
            pltpu.VMEM((count, channels), BF16),
            pltpu.VMEM(forward_rows.shape, BF16),
            pltpu.VMEM((count, channels), BF16),
            pltpu.VMEM((Y, 4 * size + 16, size), BF16),
            pltpu.VMEM(b_first.shape, F32),
            pltpu.SemaphoreType.DMA((Y, 5)),
            pltpu.SemaphoreType.DMA((5,)),
        ],
        compiler_params=SMALL,
        name="first",
    )(
        *far(
            jnp.asarray(forward_rows),
            activations.reshape(count, channels),
            flat_cot,
            w_first,
            w_second,
            b_first,
        )
    )
    pieces, cot_rows, act_rows = made[:Y], made[Y], made[Y + 1]
    route = []
    for line in range(2 * Y):
        shift = line // 2 + 4 * (line % 2)
        route += [(line * Z + z, line * Z + (z + shift) % Z) for z in range(Z)]
    arrived = lax.ppermute(cot_rows, ("y", "core", "z"), route)
    weights = []
    for d in range(Y):
        piece = shifted(pieces[d], "y", d) if d else pieces[0]
        weights += [piece, shifted(piece, "core", 1)]
    act_columns = exchange(act_rows)
    kept, sent = pl.pallas_call(
        turn_core_kernel,
        in_specs=[vmem],
        out_specs=[vmem] * 2,
        out_shape=[shaped(Y, X, tile, size)] * 2,
        compiler_params=SMALL,
        name="turn_core",
    )(*near(arrived))
    arrived = shifted(sent, "core", 1)
    turned = pl.pallas_call(
        turn_x_kernel,
        in_specs=[vmem] * 2,
        out_specs=[vmem] * X,
        out_shape=[shaped(2, Y, tile, size)] * X,
        compiler_params=SMALL,
        name="turn_x",
    )(*near(kept, arrived))
    arrived = [turned[0]] + [shifted(turned[e], "x", e) for e in range(1, X)]
    turned = pl.pallas_call(
        turn_y_kernel,
        in_specs=[vmem] * X,
        out_specs=[vmem] * Y,
        out_shape=[shaped(X, 2, tile, size)] * Y,
        compiler_params=SMALL,
        name="turn_y",
    )(*near(*arrived))
    cots = [turned[0]] + [shifted(turned[d], "y", d) for d in range(1, Y)]

    tables = [jnp.asarray(table) for table in (forward_columns, inverse_columns, folds)]
    back = pl.pallas_call(
        chain_kernel,
        in_specs=[vmem] * (4 + X) + [hbm] * sections,
        out_specs=vmem,
        out_shape=shaped(*blocks),
        scratch_shapes=[
            pltpu.VMEM((Z, X, tile, size), BF16),
            pltpu.VMEM((sections, 4 * size + 16, size), BF16),
            pltpu.SemaphoreType.DMA((sections,)),
        ],
        compiler_params=TIGHT,
        name="chain",
    )(*near(act_columns, *tables, *cots), *far(*weights))
    grads = pl.pallas_call(
        inverse_kernel,
        in_specs=[vmem] * 3,
        out_specs=hbm,
        out_shape=jax.ShapeDtypeStruct((count, channels), BF16),
        scratch_shapes=[pltpu.VMEM((count, channels), BF16), pltpu.SemaphoreType.DMA((sections,))],
        compiler_params=SMALL,
        name="inverse_rows",
    )(*near(jnp.asarray(inverse_rows), exchange(back), flat_cot))
    return grads.reshape(1, rows, width, channels)


def solution(mesh):
    chips = Mesh(mesh.devices.reshape(Y, 2, X, Z), ("y", "core", "x", "z"))
    pipe, space = ("y", "core"), ("x", "z")
    in_specs = (
        P(pipe, space, None, None),
        P(space, None, None),
        P(pipe, None, None, None, None),
        P(pipe, None, None, None, None),
        P(pipe, None, None),
    )
    out_specs = P(pipe, space, None, None)
    return jax.shard_map(body, mesh=chips, in_specs=in_specs, out_specs=out_specs, check_vma=False)
```

```python
import math

import jax
import jax.numpy as jnp
import numpy as np
from jax import lax
from jax.experimental import pallas as pl
from jax.experimental.pallas import tpu as pltpu
from jax.sharding import Mesh
from jax.sharding import PartitionSpec as P


BF16 = jnp.bfloat16
F32 = jnp.float32
X, Y, Z = 4, 4, 8
SMALL = pltpu.CompilerParams(vmem_limit_bytes=20 << 20)
TIGHT = pltpu.CompilerParams(vmem_limit_bytes=20 << 20)
EVERYONE = ("z", "core", "x", "y")


def two_parts(table):
    high = table.astype(np.float32).astype(BF16)
    low = (table - high.astype(np.float64)).astype(np.float32).astype(BF16)
    return np.concatenate([high, low], axis=1)


def row_matrix(rows, width, columns):
    modes = width // 2
    pair = modes // columns
    angles = 2.0 * math.pi * (np.outer(np.arange(modes), np.arange(width)) % width) / width
    scale = 1.0 / math.sqrt(width)
    parts = np.stack([np.cos(angles), -np.sin(angles)]) * scale
    table = np.zeros((columns, rows, 2, pair, rows, width))
    by_column = parts.reshape(2, columns, pair, width).transpose(1, 0, 2, 3)
    for h in range(rows):
        table[:, h, :, :, h, :] = by_column
    return table.reshape(columns * rows * 2 * pair, rows * width)


def column_matrix(height, pair):
    angles = 2.0 * math.pi * (np.outer(np.arange(height), np.arange(height)) % height) / height
    scale = 1.0 / math.sqrt(height)
    cosines, sines = np.cos(angles) * scale, np.sin(angles) * scale
    table = np.zeros((2, pair, height, height, 2, pair))
    for k in range(pair):
        table[0, k, :, :, 0, k] = cosines
        table[0, k, :, :, 1, k] = sines
        table[1, k, :, :, 1, k] = cosines
        table[1, k, :, :, 0, k] = -sines
    return table.reshape(2 * pair * height, 2 * pair * height)


def fold_matrices(height, pair):
    size = 2 * pair * height
    plain = np.eye(size)
    folded = np.eye(size).reshape(2, pair, height, 2, pair, height)
    eye = np.eye(height)
    flip = eye[(-np.arange(height)) % height]
    folded[0, 0, :, 0, 0, :] = 0.5 * (eye + flip)
    folded[1, 0, :, 1, 0, :] = 0.5 * (eye - flip)
    return np.stack([plain, folded.reshape(size, size)]).astype(np.float32).astype(BF16)


def dot(left, right):
    return jnp.dot(left, right, preferred_element_type=F32)


def dot_t(left, right):
    return lax.dot_general(left, right, (((1,), (1,)), ((), ())), preferred_element_type=F32)


def gelu_slope(values):
    return (
        0.5 * (1.0 + lax.erf(values * 0.7071067811865476))
        + values * jnp.exp(-0.5 * values * values) * 0.3989422804014327
    )


def twice(table_ref, operand):
    depth = operand.shape[0]
    return dot(table_ref[:, :depth], operand) + dot(table_ref[:, depth:], operand)


def first_kernel(table_hbm, act_hbm, cot_hbm, first_ref, second_ref, bias_hbm, *rest):
    pieces, cot_rows_ref, rows_ref = rest[:Y], rest[Y], rest[Y + 1]
    part, field, table_ref, act_ref, held, biases, sems, own_sems = rest[Y + 2 :]
    size = held.shape[2]
    y, core, z, odd = (*(lax.axis_index(name) for name in ("y", "core", "z")), lax.axis_index("x") & 1)
    target = (z + y + 4 * core) & (Z - 1)
    lines = part.shape[0]
    pairs = [
        (table_hbm.at[pl.ds(target * lines, lines)], part),
        (cot_hbm, field),
        (table_hbm, table_ref),
        (act_hbm, act_ref),
        (bias_hbm, biases),
    ]
    own = []
    for k, (source, place) in enumerate(pairs):
        copy = pltpu.make_async_copy(source, place, own_sems.at[k])
        copy.start()
        own.append(copy)
    loads = []
    for d in range(Y):
        block = ((y + d) & (Y - 1)) * 2 + odd
        for i in range(2):
            for j, ref in enumerate((first_ref, second_ref)):
                copy = pltpu.make_async_copy(
                    ref.at[0, i, block],
                    held.at[d, pl.ds((2 * j + i) * size, size)],
                    sems.at[d, 2 * j + i],
                )
                copy.start()
                loads.append(copy)

    depth = table_ref.shape[1] // 2
    line = lax.broadcasted_iota(jnp.int32, (lines, size), 0)
    zero_mode = jnp.logical_and(jnp.logical_and(line < 8, (line & 1) == 0), target == 0)
    factor = jnp.where(zero_mode, 1.0, 2.0).astype(F32)
    for copy in own[:2]:
        copy.wait()
    rows = jnp.concatenate([part[:, :depth], part[:, depth:]], axis=0)
    for n in range(2 * Y):
        spectrum = dot(rows, field[:, n * size : (n + 1) * size])
        tiles = ((spectrum[:lines] + spectrum[lines:]) * factor).astype(BF16)
        for i in range(2):
            for m in range(2):
                cot_rows_ref[i, n // 2, 2 * m + n % 2] = tiles[(2 * i + m) * 8 : (2 * i + m + 1) * 8]

    def transform(n):
        spectrum = twice(table_ref, act_ref[:, n * size : (n + 1) * size]).astype(BF16)
        rows_ref[:, :, :, n % 2, n // 2] = spectrum.reshape(Z, 2, 2, 8, size)

    for copy in own[2:]:
        copy.wait()
    for n in range(3):
        transform(n)
    for d in range(Y):
        block = ((y + d) & (Y - 1)) * 2 + odd
        bias = biases[0, :, pl.ds(block * size, size)]
        high = bias.astype(BF16).astype(F32)
        middle = (bias - high).astype(BF16).astype(F32)
        low = bias - high - middle
        packed = jnp.concatenate([high, middle, low, jnp.zeros((10, size), F32)], axis=0)
        held[d, 4 * size : 4 * size + 16] = packed.astype(BF16)
    for copy in loads:
        copy.wait()
    stores = []
    for d in range(Y):
        copy = pltpu.make_async_copy(held.at[d], pieces[d], sems.at[d, 4])
        copy.start()
        stores.append(copy)
    for n in range(3, 2 * Y):
        transform(n)
    for copy in stores:
        copy.wait()


def turn_core_kernel(arrived_ref, kept_ref, sent_ref):
    core = lax.axis_index("core")
    kept_ref[...] = arrived_ref[core]
    sent_ref[...] = arrived_ref[1 - core]


def turn_x_kernel(kept_ref, arrived_ref, *outs):
    x, core = lax.axis_index("x"), lax.axis_index("core")
    for e in range(X):
        to = (x + e) & (X - 1)
        outs[e][core] = kept_ref[:, to]
        outs[e][1 - core] = arrived_ref[:, to]


def turn_y_kernel(*refs):
    arrived, outs = refs[:X], refs[X:]
    y = lax.axis_index("y")
    for d in range(Y):
        for e in range(X):
            outs[d][e] = arrived[e][:, (y + d) & (Y - 1)]


def inverse_kernel(table_ref, spec_ref, cot_ref, out_ref, result, sems):
    rows = table_ref.shape[0]
    size = spec_ref.shape[6]
    copies = []
    for n in range(2 * Y):
        block = slice(n * size, (n + 1) * size)
        field = twice(table_ref, spec_ref[:, :, :, n % 2, n // 2].reshape(rows, size))
        result[:, block] = (field + cot_ref[:, block].astype(F32)).astype(BF16)
        copy = pltpu.make_async_copy(result.at[:, block], out_ref.at[:, block], sems.at[n])
        copy.start()
        copies.append(copy)
    for copy in copies:
        copy.wait()


def chain_kernel(act_ref, col_ref, inv_ref, fold_ref, *rest):
    sections = 2 * Y
    cots, weights = rest[:X], rest[X : X + sections]
    out_ref, found, held, sems = rest[X + sections :]
    size = act_ref.shape[6]
    half = col_ref.shape[0] // 2
    y, core, x, z = (lax.axis_index(name) for name in ("y", "core", "x", "z"))

    def load(p, source):
        return pltpu.make_async_copy(weights[source], held.at[p], sems.at[p])

    for here in range(sections):

        @pl.when(y * 2 + core == here)
        def _():
            for p in range(sections - 1, -1, -1):
                load(p, 2 * ((here // 2 - p // 2) % Y) + (p % 2 != here % 2)).start()

    for d in range(Y):
        for e in range(X):
            for i in range(2):
                found[(z - ((y - d) & (Y - 1)) - 4 * i) & (Z - 1), (x - e) & (X - 1)] = cots[d][e, i]
    has_zero = jnp.logical_and(jnp.logical_and(core == 0, x < 2), z == 0)
    fold = jnp.where(has_zero, 1, 0)

    base = twice(col_ref, found[...].reshape(2 * half, size))
    total = jnp.zeros_like(base)
    height_total = jnp.zeros_like(base)
    grad = base.astype(BF16)
    spectra = []
    for p in range(sections):
        columns = act_ref[:, p % 2, :, :, p // 2].reshape(2 * half, size)
        spectra.append(twice(col_ref, columns).astype(BF16))

    for p in range(sections - 1, -1, -1):
        load(p, 0).wait()
        a_re, a_im = held[p, 0:size], held[p, size : 2 * size]
        b_re, b_im = held[p, 2 * size : 3 * size], held[p, 3 * size : 4 * size]
        bias = held[p, 4 * size : 4 * size + 16].astype(F32)
        bias_re = bias[0:1] + bias[2:3] + bias[4:5]
        bias_im = bias[1:2] + bias[3:4] + bias[5:6]
        s = spectra[p]
        s_turned = jnp.concatenate([-s[half:], s[:half]], axis=0)
        z_both = dot(s, a_re) + dot(s_turned, a_im)
        slope = gelu_slope(jnp.concatenate([z_both[:half] + bias_re, z_both[half:] + bias_im], axis=0))
        g_turned = jnp.concatenate([grad[half:], -grad[:half]], axis=0)
        u = dot_t(grad, b_re) + dot_t(g_turned, b_im)
        q = (u * slope).astype(BF16)
        q_turned = jnp.concatenate([q[half:], -q[:half]], axis=0)
        e = (dot_t(q, a_re) + dot_t(q_turned, a_im)).astype(BF16)
        height_total = height_total + twice(inv_ref, e)
        out_ref[:, p % 2, :, :, p // 2] = height_total.astype(BF16).reshape(Z, 2, 2, 8, size)
        if p > 0:
            total = total + dot(fold_ref[fold], e)
            grad = (base + total).astype(BF16)


def body(activations, cotangent, w_first, w_second, b_first):
    sections, columns = 2 * Y, X * Z
    _, rows, width, channels = activations.shape
    size = w_first.shape[3]
    height = rows * columns
    pair = width // 2 // columns
    count = rows * width
    tile = 2 * rows * pair
    row_table = row_matrix(rows, width, columns)
    row_table = row_table.reshape(2, 2, Z, -1).transpose(2, 0, 1, 3).reshape(row_table.shape)
    forward_rows, inverse_rows = two_parts(row_table), two_parts(row_table.T)
    column_table = column_matrix(height, pair)
    column_table = column_table.reshape(-1, X, Z, tile).transpose(0, 2, 1, 3).reshape(column_table.shape)
    forward_columns, inverse_columns = two_parts(column_table), two_parts(column_table.T)
    folds = fold_matrices(height, pair)

    vmem = pl.BlockSpec(memory_space=pltpu.VMEM)
    hbm = pl.BlockSpec(memory_space=pl.ANY)
    blocks = (Z, 2, 2, 2, Y, tile, size)

    def shaped(*dims):
        return pltpu.VMEM(dims, BF16)

    def near(*values):
        return [pltpu.with_memory_space_constraint(value, pltpu.VMEM) for value in values]

    def far(*values):
        return [pltpu.with_memory_space_constraint(value, pltpu.HBM) for value in values]

    def exchange(value):
        flat = value.reshape(sections * columns, tile, size)
        return lax.all_to_all(flat, EVERYONE, split_axis=0, concat_axis=0, tiled=True).reshape(blocks)

    def shifted(value, axis, distance):
        size = lax.axis_size(axis)
        return lax.ppermute(value, axis, [(i, (i + distance) % size) for i in range(size)])

    flat_cot = cotangent.reshape(count, channels)
    made = pl.pallas_call(
        first_kernel,
        in_specs=[hbm] * 6,
        out_specs=[hbm] * Y + [vmem] * 2,
        out_shape=[pltpu.HBM((4 * size + 16, size), BF16)] * Y + [shaped(2, Y, X, tile, size), shaped(*blocks)],
        scratch_shapes=[
            pltpu.VMEM((4 * tile, 2 * count), BF16),
            pltpu.VMEM((count, channels), BF16),
            pltpu.VMEM(forward_rows.shape, BF16),
            pltpu.VMEM((count, channels), BF16),
            pltpu.VMEM((Y, 4 * size + 16, size), BF16),
            pltpu.VMEM(b_first.shape, F32),
            pltpu.SemaphoreType.DMA((Y, 5)),
            pltpu.SemaphoreType.DMA((5,)),
        ],
        compiler_params=SMALL,
        name="first",
    )(
        *far(
            jnp.asarray(forward_rows),
            activations.reshape(count, channels),
            flat_cot,
            w_first,
            w_second,
            b_first,
        )
    )
    pieces, cot_rows, act_rows = made[:Y], made[Y], made[Y + 1]
    route = []
    for line in range(2 * Y):
        shift = line // 2 + 4 * (line % 2)
        route += [(line * Z + z, line * Z + (z + shift) % Z) for z in range(Z)]
    arrived = lax.ppermute(cot_rows, ("y", "core", "z"), route)
    weights = []
    for d in range(Y):
        piece = shifted(pieces[d], "y", d) if d else pieces[0]
        weights += [piece, shifted(piece, "core", 1)]
    act_columns = exchange(act_rows)
    kept, sent = pl.pallas_call(
        turn_core_kernel,
        in_specs=[vmem],
        out_specs=[vmem] * 2,
        out_shape=[shaped(Y, X, tile, size)] * 2,
        compiler_params=SMALL,
        name="turn_core",
    )(*near(arrived))
    arrived = shifted(sent, "core", 1)
    turned = pl.pallas_call(
        turn_x_kernel,
        in_specs=[vmem] * 2,
        out_specs=[vmem] * X,
        out_shape=[shaped(2, Y, tile, size)] * X,
        compiler_params=SMALL,
        name="turn_x",
    )(*near(kept, arrived))
    arrived = [turned[0]] + [shifted(turned[e], "x", e) for e in range(1, X)]
    turned = pl.pallas_call(
        turn_y_kernel,
        in_specs=[vmem] * X,
        out_specs=[vmem] * Y,
        out_shape=[shaped(X, 2, tile, size)] * Y,
        compiler_params=SMALL,
        name="turn_y",
    )(*near(*arrived))
    cots = [turned[0]] + [shifted(turned[d], "y", d) for d in range(1, Y)]

    tables = [jnp.asarray(table) for table in (forward_columns, inverse_columns, folds)]
    back = pl.pallas_call(
        chain_kernel,
        in_specs=[vmem] * (4 + X) + [hbm] * sections,
        out_specs=vmem,
        out_shape=shaped(*blocks),
        scratch_shapes=[
            pltpu.VMEM((Z, X, tile, size), BF16),
            pltpu.VMEM((sections, 4 * size + 16, size), BF16),
            pltpu.SemaphoreType.DMA((sections,)),
        ],
        compiler_params=TIGHT,
        name="chain",
    )(*near(act_columns, *tables, *cots), *far(*weights))
    grads = pl.pallas_call(
        inverse_kernel,
        in_specs=[vmem] * 3,
        out_specs=hbm,
        out_shape=jax.ShapeDtypeStruct((count, channels), BF16),
        scratch_shapes=[pltpu.VMEM((count, channels), BF16), pltpu.SemaphoreType.DMA((sections,))],
        compiler_params=SMALL,
        name="inverse_rows",
    )(*near(jnp.asarray(inverse_rows), exchange(back), flat_cot))
    return grads.reshape(1, rows, width, channels)


def solution(mesh):
    chips = Mesh(mesh.devices.reshape(Y, 2, X, Z), ("y", "core", "x", "z"))
    pipe, space = ("y", "core"), ("x", "z")
    in_specs = (
        P(pipe, space, None, None),
        P(space, None, None),
        P(pipe, None, None, None, None),
        P(pipe, None, None, None, None),
        P(pipe, None, None),
    )
    out_specs = P(pipe, space, None, None)
    return jax.shard_map(body, mesh=chips, in_specs=in_specs, out_specs=out_specs, check_vma=False)
```

```python
import math

import jax
import jax.numpy as jnp
import numpy as np
from jax import lax
from jax.experimental import pallas as pl
from jax.experimental.pallas import tpu as pltpu
from jax.sharding import Mesh
from jax.sharding import PartitionSpec as P


BF16 = jnp.bfloat16
F32 = jnp.float32
X, Y, Z = 4, 4, 8
SMALL = pltpu.CompilerParams(vmem_limit_bytes=20 << 20)
TIGHT = pltpu.CompilerParams(vmem_limit_bytes=20 << 20)
EVERYONE = ("z", "core", "x", "y")


def two_parts(table):
    high = table.astype(np.float32).astype(BF16)
    low = (table - high.astype(np.float64)).astype(np.float32).astype(BF16)
    return np.concatenate([high, low], axis=1)


def row_matrix(rows, width, columns):
    modes = width // 2
    pair = modes // columns
    angles = 2.0 * math.pi * (np.outer(np.arange(modes), np.arange(width)) % width) / width
    scale = 1.0 / math.sqrt(width)
    parts = np.stack([np.cos(angles), -np.sin(angles)]) * scale
    table = np.zeros((columns, rows, 2, pair, rows, width))
    by_column = parts.reshape(2, columns, pair, width).transpose(1, 0, 2, 3)
    for h in range(rows):
        table[:, h, :, :, h, :] = by_column
    return table.reshape(columns * rows * 2 * pair, rows * width)


def column_matrix(height, pair):
    angles = 2.0 * math.pi * (np.outer(np.arange(height), np.arange(height)) % height) / height
    scale = 1.0 / math.sqrt(height)
    cosines, sines = np.cos(angles) * scale, np.sin(angles) * scale
    table = np.zeros((2, pair, height, height, 2, pair))
    for k in range(pair):
        table[0, k, :, :, 0, k] = cosines
        table[0, k, :, :, 1, k] = sines
        table[1, k, :, :, 1, k] = cosines
        table[1, k, :, :, 0, k] = -sines
    return table.reshape(2 * pair * height, 2 * pair * height)


def fold_matrices(height, pair):
    size = 2 * pair * height
    plain = np.eye(size)
    folded = np.eye(size).reshape(2, pair, height, 2, pair, height)
    eye = np.eye(height)
    flip = eye[(-np.arange(height)) % height]
    folded[0, 0, :, 0, 0, :] = 0.5 * (eye + flip)
    folded[1, 0, :, 1, 0, :] = 0.5 * (eye - flip)
    return np.stack([plain, folded.reshape(size, size)]).astype(np.float32).astype(BF16)


def dot(left, right):
    return jnp.dot(left, right, preferred_element_type=F32)


def dot_t(left, right):
    return lax.dot_general(left, right, (((1,), (1,)), ((), ())), preferred_element_type=F32)


def gelu_slope(values):
    return (
        0.5 * (1.0 + lax.erf(values * 0.7071067811865476))
        + values * jnp.exp(-0.5 * values * values) * 0.3989422804014327
    )


def twice(table_ref, operand):
    depth = operand.shape[0]
    return dot(table_ref[:, :depth], operand) + dot(table_ref[:, depth:], operand)


def first_kernel(table_hbm, act_hbm, cot_hbm, first_ref, second_ref, bias_hbm, *rest):
    pieces, cot_rows_ref, rows_ref = rest[:Y], rest[Y], rest[Y + 1]
    part, field, table_ref, act_ref, held, biases, sems, own_sems = rest[Y + 2 :]
    size = held.shape[2]
    y, core, z, odd = (*(lax.axis_index(name) for name in ("y", "core", "z")), lax.axis_index("x") & 1)
    target = (z + y + 4 * core) & (Z - 1)
    lines = part.shape[0]
    pairs = [
        (table_hbm.at[pl.ds(target * lines, lines)], part),
        (cot_hbm, field),
        (table_hbm, table_ref),
        (act_hbm, act_ref),
        (bias_hbm, biases),
    ]
    loads = []
    for d in range(Y):
        block = ((y + d) & (Y - 1)) * 2 + odd
        for i in range(2):
            for j, ref in enumerate((first_ref, second_ref)):
                copy = pltpu.make_async_copy(
                    ref.at[0, i, block],
                    held.at[d, pl.ds((2 * j + i) * size, size)],
                    sems.at[d, 2 * j + i],
                )
                copy.start()
                loads.append(copy)
    own = []
    for k, (source, place) in enumerate(pairs):
        copy = pltpu.make_async_copy(source, place, own_sems.at[k])
        copy.start()
        own.append(copy)

    depth = table_ref.shape[1] // 2
    line = lax.broadcasted_iota(jnp.int32, (lines, size), 0)
    zero_mode = jnp.logical_and(jnp.logical_and(line < 8, (line & 1) == 0), target == 0)
    factor = jnp.where(zero_mode, 1.0, 2.0).astype(F32)
    for copy in own[:2]:
        copy.wait()
    rows = jnp.concatenate([part[:, :depth], part[:, depth:]], axis=0)
    for n in range(2 * Y):
        spectrum = dot(rows, field[:, n * size : (n + 1) * size])
        tiles = ((spectrum[:lines] + spectrum[lines:]) * factor).astype(BF16)
        for i in range(2):
            for m in range(2):
                cot_rows_ref[i, n // 2, 2 * m + n % 2] = tiles[(2 * i + m) * 8 : (2 * i + m + 1) * 8]

    for copy in own[2:]:
        copy.wait()
    for d in range(Y):
        block = ((y + d) & (Y - 1)) * 2 + odd
        bias = biases[0, :, pl.ds(block * size, size)]
        high = bias.astype(BF16).astype(F32)
        middle = (bias - high).astype(BF16).astype(F32)
        low = bias - high - middle
        packed = jnp.concatenate([high, middle, low, jnp.zeros((10, size), F32)], axis=0)
        held[d, 4 * size : 4 * size + 16] = packed.astype(BF16)
    stores = []
    for d in range(Y):
        for copy in loads[4 * d : 4 * d + 4]:
            copy.wait()
        copy = pltpu.make_async_copy(held.at[d], pieces[d], sems.at[d, 4])
        copy.start()
        stores.append(copy)
    for n in range(2 * Y):
        spectrum = twice(table_ref, act_ref[:, n * size : (n + 1) * size]).astype(BF16)
        rows_ref[:, :, :, n % 2, n // 2] = spectrum.reshape(Z, 2, 2, 8, size)
    for copy in stores:
        copy.wait()


def turn_core_kernel(arrived_ref, kept_ref, sent_ref):
    core = lax.axis_index("core")
    kept_ref[...] = arrived_ref[core]
    sent_ref[...] = arrived_ref[1 - core]


def turn_x_kernel(kept_ref, arrived_ref, *outs):
    x, core = lax.axis_index("x"), lax.axis_index("core")
    for e in range(X):
        to = (x + e) & (X - 1)
        outs[e][core] = kept_ref[:, to]
        outs[e][1 - core] = arrived_ref[:, to]


def turn_y_kernel(*refs):
    arrived, outs = refs[:X], refs[X:]
    y = lax.axis_index("y")
    for d in range(Y):
        for e in range(X):
            outs[d][e] = arrived[e][:, (y + d) & (Y - 1)]


def inverse_kernel(table_ref, spec_ref, cot_ref, out_ref, result, sems):
    rows = table_ref.shape[0]
    size = spec_ref.shape[6]
    copies = []
    for n in range(2 * Y):
        block = slice(n * size, (n + 1) * size)
        field = twice(table_ref, spec_ref[:, :, :, n % 2, n // 2].reshape(rows, size))
        result[:, block] = (field + cot_ref[:, block].astype(F32)).astype(BF16)
        copy = pltpu.make_async_copy(result.at[:, block], out_ref.at[:, block], sems.at[n])
        copy.start()
        copies.append(copy)
    for copy in copies:
        copy.wait()


def chain_kernel(act_ref, col_ref, inv_ref, fold_ref, *rest):
    sections = 2 * Y
    cots, weights = rest[:X], rest[X : X + sections]
    out_ref, found, held, sems = rest[X + sections :]
    size = act_ref.shape[6]
    half = col_ref.shape[0] // 2
    y, core, x, z = (lax.axis_index(name) for name in ("y", "core", "x", "z"))

    def load(p, source):
        return pltpu.make_async_copy(weights[source], held.at[p], sems.at[p])

    for here in range(sections):

        @pl.when(y * 2 + core == here)
        def _():
            for p in range(sections - 1, -1, -1):
                load(p, 2 * ((here // 2 - p // 2) % Y) + (p % 2 != here % 2)).start()

    for d in range(Y):
        for e in range(X):
            for i in range(2):
                found[(z - ((y - d) & (Y - 1)) - 4 * i) & (Z - 1), (x - e) & (X - 1)] = cots[d][e, i]
    has_zero = jnp.logical_and(jnp.logical_and(core == 0, x < 2), z == 0)
    fold = jnp.where(has_zero, 1, 0)

    base = twice(col_ref, found[...].reshape(2 * half, size))
    total = jnp.zeros_like(base)
    height_total = jnp.zeros_like(base)
    grad = base.astype(BF16)
    spectra = []
    for p in range(sections):
        columns = act_ref[:, p % 2, :, :, p // 2].reshape(2 * half, size)
        spectra.append(twice(col_ref, columns).astype(BF16))

    for p in range(sections - 1, -1, -1):
        load(p, 0).wait()
        a_re, a_im = held[p, 0:size], held[p, size : 2 * size]
        b_re, b_im = held[p, 2 * size : 3 * size], held[p, 3 * size : 4 * size]
        bias = held[p, 4 * size : 4 * size + 16].astype(F32)
        bias_re = bias[0:1] + bias[2:3] + bias[4:5]
        bias_im = bias[1:2] + bias[3:4] + bias[5:6]
        s = spectra[p]
        s_turned = jnp.concatenate([-s[half:], s[:half]], axis=0)
        z_both = dot(s, a_re) + dot(s_turned, a_im)
        slope = gelu_slope(jnp.concatenate([z_both[:half] + bias_re, z_both[half:] + bias_im], axis=0))
        g_turned = jnp.concatenate([grad[half:], -grad[:half]], axis=0)
        u = dot_t(grad, b_re) + dot_t(g_turned, b_im)
        q = (u * slope).astype(BF16)
        q_turned = jnp.concatenate([q[half:], -q[:half]], axis=0)
        e = (dot_t(q, a_re) + dot_t(q_turned, a_im)).astype(BF16)
        height_total = height_total + twice(inv_ref, e)
        out_ref[:, p % 2, :, :, p // 2] = height_total.astype(BF16).reshape(Z, 2, 2, 8, size)
        if p > 0:
            total = total + dot(fold_ref[fold], e)
            grad = (base + total).astype(BF16)


def body(activations, cotangent, w_first, w_second, b_first):
    sections, columns = 2 * Y, X * Z
    _, rows, width, channels = activations.shape
    size = w_first.shape[3]
    height = rows * columns
    pair = width // 2 // columns
    count = rows * width
    tile = 2 * rows * pair
    row_table = row_matrix(rows, width, columns)
    row_table = row_table.reshape(2, 2, Z, -1).transpose(2, 0, 1, 3).reshape(row_table.shape)
    forward_rows, inverse_rows = two_parts(row_table), two_parts(row_table.T)
    column_table = column_matrix(height, pair)
    column_table = column_table.reshape(-1, X, Z, tile).transpose(0, 2, 1, 3).reshape(column_table.shape)
    forward_columns, inverse_columns = two_parts(column_table), two_parts(column_table.T)
    folds = fold_matrices(height, pair)

    vmem = pl.BlockSpec(memory_space=pltpu.VMEM)
    hbm = pl.BlockSpec(memory_space=pl.ANY)
    blocks = (Z, 2, 2, 2, Y, tile, size)

    def shaped(*dims):
        return pltpu.VMEM(dims, BF16)

    def near(*values):
        return [pltpu.with_memory_space_constraint(value, pltpu.VMEM) for value in values]

    def far(*values):
        return [pltpu.with_memory_space_constraint(value, pltpu.HBM) for value in values]

    def exchange(value):
        flat = value.reshape(sections * columns, tile, size)
        return lax.all_to_all(flat, EVERYONE, split_axis=0, concat_axis=0, tiled=True).reshape(blocks)

    def shifted(value, axis, distance):
        size = lax.axis_size(axis)
        return lax.ppermute(value, axis, [(i, (i + distance) % size) for i in range(size)])

    flat_cot = cotangent.reshape(count, channels)
    made = pl.pallas_call(
        first_kernel,
        in_specs=[hbm] * 6,
        out_specs=[hbm] * Y + [vmem] * 2,
        out_shape=[pltpu.HBM((4 * size + 16, size), BF16)] * Y + [shaped(2, Y, X, tile, size), shaped(*blocks)],
        scratch_shapes=[
            pltpu.VMEM((4 * tile, 2 * count), BF16),
            pltpu.VMEM((count, channels), BF16),
            pltpu.VMEM(forward_rows.shape, BF16),
            pltpu.VMEM((count, channels), BF16),
            pltpu.VMEM((Y, 4 * size + 16, size), BF16),
            pltpu.VMEM(b_first.shape, F32),
            pltpu.SemaphoreType.DMA((Y, 5)),
            pltpu.SemaphoreType.DMA((5,)),
        ],
        compiler_params=SMALL,
        name="first",
    )(
        *far(
            jnp.asarray(forward_rows),
            activations.reshape(count, channels),
            flat_cot,
            w_first,
            w_second,
            b_first,
        )
    )
    pieces, cot_rows, act_rows = made[:Y], made[Y], made[Y + 1]
    route = []
    for line in range(2 * Y):
        shift = line // 2 + 4 * (line % 2)
        route += [(line * Z + z, line * Z + (z + shift) % Z) for z in range(Z)]
    arrived = lax.ppermute(cot_rows, ("y", "core", "z"), route)
    weights = []
    for d in range(Y):
        piece = shifted(pieces[d], "y", d) if d else pieces[0]
        weights += [piece, shifted(piece, "core", 1)]
    act_columns = exchange(act_rows)
    kept, sent = pl.pallas_call(
        turn_core_kernel,
        in_specs=[vmem],
        out_specs=[vmem] * 2,
        out_shape=[shaped(Y, X, tile, size)] * 2,
        compiler_params=SMALL,
        name="turn_core",
    )(*near(arrived))
    arrived = shifted(sent, "core", 1)
    turned = pl.pallas_call(
        turn_x_kernel,
        in_specs=[vmem] * 2,
        out_specs=[vmem] * X,
        out_shape=[shaped(2, Y, tile, size)] * X,
        compiler_params=SMALL,
        name="turn_x",
    )(*near(kept, arrived))
    arrived = [turned[0]] + [shifted(turned[e], "x", e) for e in range(1, X)]
    turned = pl.pallas_call(
        turn_y_kernel,
        in_specs=[vmem] * X,
        out_specs=[vmem] * Y,
        out_shape=[shaped(X, 2, tile, size)] * Y,
        compiler_params=SMALL,
        name="turn_y",
    )(*near(*arrived))
    cots = [turned[0]] + [shifted(turned[d], "y", d) for d in range(1, Y)]

    tables = [jnp.asarray(table) for table in (forward_columns, inverse_columns, folds)]
    back = pl.pallas_call(
        chain_kernel,
        in_specs=[vmem] * (4 + X) + [hbm] * sections,
        out_specs=vmem,
        out_shape=shaped(*blocks),
        scratch_shapes=[
            pltpu.VMEM((Z, X, tile, size), BF16),
            pltpu.VMEM((sections, 4 * size + 16, size), BF16),
            pltpu.SemaphoreType.DMA((sections,)),
        ],
        compiler_params=TIGHT,
        name="chain",
    )(*near(act_columns, *tables, *cots), *far(*weights))
    grads = pl.pallas_call(
        inverse_kernel,
        in_specs=[vmem] * 3,
        out_specs=hbm,
        out_shape=jax.ShapeDtypeStruct((count, channels), BF16),
        scratch_shapes=[pltpu.VMEM((count, channels), BF16), pltpu.SemaphoreType.DMA((sections,))],
        compiler_params=SMALL,
        name="inverse_rows",
    )(*near(jnp.asarray(inverse_rows), exchange(back), flat_cot))
    return grads.reshape(1, rows, width, channels)


def solution(mesh):
    chips = Mesh(mesh.devices.reshape(Y, 2, X, Z), ("y", "core", "x", "z"))
    pipe, space = ("y", "core"), ("x", "z")
    in_specs = (
        P(pipe, space, None, None),
        P(space, None, None),
        P(pipe, None, None, None, None),
        P(pipe, None, None, None, None),
        P(pipe, None, None),
    )
    out_specs = P(pipe, space, None, None)
    return jax.shard_map(body, mesh=chips, in_specs=in_specs, out_specs=out_specs, check_vma=False)
```
